512 devices in a mesh: doc: 8 (over y, core), label: 64 (over z, x).
Axes of the slice: x: 4, y: 4, z: 16, core: 2. Of those that a mesh axis runs over, the one named last changes fastest.
Arguments:
- features: float32 [4096, 1024], P('doc'), may hold values from -6 to 6
- doc_labels: int32 [4096, 16], P('doc'), may hold values from 0 to 16383, all different within a row
- tree_perm: int32 [16384], replicated, may hold values from 0 to 16383, as said below
- cluster_sizes: int32 [512], replicated, may hold values from 1 to 4096, 16384 in all
Outputs:
- scores: float32 [4096, 16384], P('doc', 'label')
The draws below stay inside these ranges and needn't reach their ends.
Inputs may be any that keep to these rules, and one draw needn't show every extreme that they name: `doc_labels`: each document names 16 different labels, and every label is named by some document. `tree_perm`: a permutation; every aligned block of 256 tree positions holds exactly 4 labels of every aligned block of 256 natural indices. `cluster_sizes`: the sizes sum to 16384; the largest is exactly 4096.
All inputs are finite; a program needn't handle non-finite values.
Results may differ from the reference program's by a relative error of at most 0.0001.
Values sent between devices are 32-bit elements; how exact they have to be, the bound alone decides.
No kernel may reach another device: no remote copies, remote signals or barrier semaphores. Data moves between devices by JAX's collectives and lax.ppermute only.
A program may use at most 64 MiB of HBM per device.

```python
import math
import jax
import jax.numpy as jnp
import numpy as np
from jax import lax

D = 1024
K = 16
L_DEV = 256
DOCS = 4096
L = 16384
PER_PAIR = 4
NC = 512
MOST = 4096


def draw_tree_perm(key, part):
    blocks = L // L_DEV
    keys = jax.random.split(key, 2 * blocks)
    sigma = jax.vmap(lambda k: jax.random.permutation(k, L_DEV))(keys[:blocks]).astype(jnp.int32)
    tau = jax.vmap(lambda k: jax.random.permutation(k, L_DEV))(keys[blocks:]).astype(jnp.int32)
    source = jnp.arange(blocks, dtype=jnp.int32)[:, None]
    dest = sigma // PER_PAIR
    slot = source * PER_PAIR + sigma % PER_PAIR
    position = dest * L_DEV + tau[dest, slot]
    return jnp.argsort(position.reshape(L)).astype(jnp.int32)


def block_levels(key, extent, cuts, least, top_value):
    factor_of, own = 1.0, jax.random.fold_in(key, 6)
    for axis_at, parts in cuts:
        draws = jnp.exp(jax.random.uniform(jax.random.fold_in(own, axis_at), (parts,), jnp.float32, least / len(cuts), top_value / len(cuts)))
        factor_of = factor_of * jnp.repeat(draws, extent[axis_at] // parts).reshape([-1 if axis == axis_at else 1 for axis in range(len(extent))])
    return factor_of


def distinct(own_key, rows, amount, top, lift):
    ranking = jax.random.permutation(jax.random.fold_in(own_key, 1), amount)
    favour = ranking
    for power in range(3):
        favour = favour * favour // amount
    favour = favour * lift // amount
    chance = jax.random.randint(jax.random.fold_in(own_key, 2), (rows, amount), 0, 4096) + favour
    sure = jax.random.permutation(jax.random.fold_in(own_key, 3), rows)[jnp.arange(amount) % rows]
    chance = jnp.where(jnp.arange(rows)[:, None] == sure[None, :], 1 << 14, chance)
    priority = chance * amount + jnp.arange(amount)
    return lax.top_k(priority.astype(jnp.int32), top)[1].astype(jnp.int32)


def profile(number_of, total, bound, skew):
    loads = [(1 << 20) // math.isqrt(grade ** skew) + 1 for grade in range(2, number_of + 1)]
    rest, holding = total - bound - (number_of - 1), [1] * (number_of - 1)
    while rest > 0:
        candidates = [i for i in range(number_of - 1) if holding[i] < bound]
        mass, budget = sum([loads[i] for i in candidates]), rest
        for i in candidates:
            extra = min(bound - holding[i], max(1, budget * loads[i] // mass), rest)
            holding[i] = holding[i] + extra
            rest = rest - extra
    return np.array([bound] + holding)


def ragged(rng, number_of, total, limit, skew):
    if number_of == 2:
        one = jax.random.randint(rng, (), max(1, total - limit), min(limit, total - 1) + 1)
        return jnp.stack([one, total - one])
    lengths = jnp.asarray(profile(number_of, total, limit, skew), jnp.int32)
    twos = (number_of - 1) // 2
    source_of, sink = lengths[1:1 + 2 * twos:2], lengths[2:2 + 2 * twos:2]
    room = jnp.minimum(source_of - 1, limit - sink)
    moved = jax.random.randint(jax.random.fold_in(rng, 1), (twos,), 0, 1 << 20) % (room + 1)
    lengths = lengths.at[1:1 + 2 * twos:2].set(source_of - moved).at[2:2 + 2 * twos:2].set(sink + moved)
    return lengths[jax.random.permutation(jax.random.fold_in(rng, 2), number_of)]


def gaussian(rng, dims, deviation, most, pieces=(), kind=jnp.bfloat16):
    entries = deviation * jax.random.normal(rng, dims, jnp.float32)
    if pieces:
        entries = entries * block_levels(rng, dims, pieces, -0.22, 0.18)
    return jnp.clip(entries, -most, most).astype(kind)


def setup_inputs(seed: int = 0) -> dict:
    arg_keys = jax.random.split(jax.random.key(seed), 5)
    features = gaussian(arg_keys[0], (DOCS, D), 1.0, 6.0, ((0, 8),), jnp.float32)
    doc_labels = distinct(arg_keys[1], DOCS, L, K, 8)
    tree_perm = draw_tree_perm(jax.random.fold_in(arg_keys[4], 71), 0)
    cluster_sizes = ragged(arg_keys[3], NC, L, MOST, 2).astype(jnp.int32)
    return {"features": features, "doc_labels": doc_labels, "tree_perm": tree_perm, "cluster_sizes": cluster_sizes}


EPS = 1e-06

def unit_rows(matrix):
    return matrix * lax.rsqrt(lax.optimization_barrier(jnp.sum(matrix * matrix, axis=1, keepdims=True)) + EPS)

def reference(features, doc_labels, tree_perm, cluster_sizes):

    def add_slot(total, column):
        return (total + jax.ops.segment_sum(features, column, num_segments=L), None)
    summed, _ = lax.scan(add_slot, jnp.zeros((L, D), jnp.float32), doc_labels.T)
    normed = unit_rows(summed)
    label_rows = normed[tree_perm]
    cluster_ids = jnp.repeat(jnp.arange(NC, dtype=jnp.int32), cluster_sizes, total_repeat_length=L)
    sums = jax.ops.segment_sum(label_rows, cluster_ids, num_segments=NC)
    centroid = unit_rows(sums)[cluster_ids]
    combined = label_rows + centroid
    doc_unit = unit_rows(features)
    return lax.dot_general(doc_unit, combined, (((1,), (1,)), ((), ())), precision=lax.Precision.HIGHEST, preferred_element_type=jnp.float32)
```

```python
import jax
import jax.numpy as jnp
from jax import lax
from jax.sharding import PartitionSpec as P

L_DEV = 256


EPS = 1e-06


def unit_rows(matrix):
    return matrix * lax.rsqrt(jnp.sum(matrix * matrix, axis=1, keepdims=True) + EPS)


def cluster_of(positions, starts):
    return jnp.sum((starts[None, 1:] <= positions[:, None]).astype(jnp.int32), axis=1)


def shards(features, doc_labels, tree_perm, cluster_sizes):
    width = lax.axis_size("label")
    here = lax.axis_index("label")
    base = here * L_DEV
    slots = jnp.arange(L_DEV, dtype=jnp.int32)

    own_perm = lax.dynamic_slice_in_dim(tree_perm, base, L_DEV)
    incidence = jnp.sum(
        (doc_labels[:, :, None] == own_perm[None, None, :]).astype(jnp.float32), axis=1
    )
    partial_value = lax.dot_general(
        incidence,
        features,
        (((0,), (0,)), ((), ())),
        precision=lax.Precision.HIGHEST,
        preferred_element_type=jnp.float32,
    )
    summed = lax.psum(partial_value, "doc")
    label_rows = unit_rows(summed)

    starts = jnp.cumsum(cluster_sizes) - cluster_sizes
    cluster_ids = cluster_of(base + slots, starts)
    shard = jnp.arange(width, dtype=jnp.int32)
    first_id = cluster_of(shard * L_DEV, starts)
    last_id = cluster_of(shard * L_DEV + (L_DEV - 1), starts)

    same_cluster = (cluster_ids[:, None] == cluster_ids[None, :]).astype(jnp.float32)
    local_sum = jnp.dot(
        same_cluster,
        label_rows,
        precision=lax.Precision.HIGHEST,
        preferred_element_type=jnp.float32,
    )
    ends = jnp.stack([local_sum[0], local_sum[-1]])
    gathered = lax.all_gather(ends, "label").reshape(2 * width, -1)

    other = (shard != here)[None, :]
    take_first = (first_id[None, :] == cluster_ids[:, None]) & other
    take_last = (last_id[None, :] == cluster_ids[:, None]) & (first_id != last_id)[None, :] & other
    weights = jnp.stack([take_first, take_last], axis=2).reshape(L_DEV, 2 * width)
    cluster_sum = local_sum + jnp.dot(
        weights.astype(jnp.float32),
        gathered,
        precision=lax.Precision.HIGHEST,
        preferred_element_type=jnp.float32,
    )
    centroid = unit_rows(cluster_sum)
    combined = label_rows + centroid
    doc_unit = unit_rows(features)
    return lax.dot_general(
        doc_unit,
        combined,
        (((1,), (1,)), ((), ())),
        precision=lax.Precision.HIGHEST,
        preferred_element_type=jnp.float32,
    )


def solution(mesh):
    in_specs = (P("doc", None), P("doc", None), P(), P())
    out_specs = P("doc", "label")
    return jax.shard_map(shards, mesh=mesh, in_specs=in_specs, out_specs=out_specs, check_vma=False)
```

```python
import jax
import jax.numpy as jnp
from jax import lax
from jax.sharding import PartitionSpec as P

L_DEV = 256


EPS = 1e-06


def unit_rows(matrix):
    return matrix * lax.rsqrt(jnp.sum(matrix * matrix, axis=1, keepdims=True) + EPS)


def cluster_of(positions, starts):
    return jnp.sum((starts[None, 1:] <= positions[:, None]).astype(jnp.int32), axis=1)


def shards(features, doc_labels, tree_perm, cluster_sizes):
    width = lax.axis_size("label")
    here = lax.axis_index("label")
    base = here * L_DEV
    slots = jnp.arange(L_DEV, dtype=jnp.int32)

    own_perm = lax.dynamic_slice_in_dim(tree_perm, base, L_DEV)
    incidence = jnp.sum(
        (doc_labels[:, :, None] == own_perm[None, None, :]).astype(jnp.float32), axis=1
    )
    partial_value = lax.dot_general(
        incidence,
        features,
        (((0,), (0,)), ((), ())),
        precision=lax.Precision.HIGHEST,
        preferred_element_type=jnp.float32,
    )
    groups = lax.axis_size("doc")
    depth = features.shape[1]
    pieces = lax.all_to_all(
        partial_value.reshape(groups, L_DEV // groups, depth), "doc", 0, 0, tiled=True
    )
    mine = unit_rows(jnp.sum(pieces, axis=0))
    label_rows = lax.all_to_all(
        jnp.broadcast_to(mine[None], (groups,) + mine.shape), "doc", 0, 0, tiled=True
    ).reshape(L_DEV, depth)

    starts = jnp.cumsum(cluster_sizes) - cluster_sizes
    cluster_ids = cluster_of(base + slots, starts)
    shard = jnp.arange(width, dtype=jnp.int32)
    first_id = cluster_of(shard * L_DEV, starts)
    last_id = cluster_of(shard * L_DEV + (L_DEV - 1), starts)

    same_cluster = (cluster_ids[:, None] == cluster_ids[None, :]).astype(jnp.float32)
    local_sum = jnp.dot(
        same_cluster,
        label_rows,
        precision=lax.Precision.HIGHEST,
        preferred_element_type=jnp.float32,
    )
    ends = jnp.stack([local_sum[0], local_sum[-1]])
    gathered = lax.all_to_all(
        jnp.broadcast_to(ends[None], (width,) + ends.shape), "label", 0, 0, tiled=True
    ).reshape(2 * width, -1)

    other = (shard != here)[None, :]
    take_first = (first_id[None, :] == cluster_ids[:, None]) & other
    take_last = (last_id[None, :] == cluster_ids[:, None]) & (first_id != last_id)[None, :] & other
    weights = jnp.stack([take_first, take_last], axis=2).reshape(L_DEV, 2 * width)
    cluster_sum = local_sum + jnp.dot(
        weights.astype(jnp.float32),
        gathered,
        precision=lax.Precision.HIGHEST,
        preferred_element_type=jnp.float32,
    )
    centroid = unit_rows(cluster_sum)
    combined = label_rows + centroid
    doc_unit = unit_rows(features)
    return lax.dot_general(
        doc_unit,
        combined,
        (((1,), (1,)), ((), ())),
        precision=lax.Precision.HIGHEST,
        preferred_element_type=jnp.float32,
    )


def solution(mesh):
    in_specs = (P("doc", None), P("doc", None), P(), P())
    out_specs = P("doc", "label")
    return jax.shard_map(shards, mesh=mesh, in_specs=in_specs, out_specs=out_specs, check_vma=False)
```

```python
import jax
import jax.numpy as jnp
from jax import lax
from jax.sharding import PartitionSpec as P

L_DEV = 256


EPS = 1e-06


def unit_rows(matrix):
    return matrix * lax.rsqrt(jnp.sum(matrix * matrix, axis=1, keepdims=True) + EPS)


def cluster_of(positions, starts):
    return jnp.sum((starts[None, 1:] <= positions[:, None]).astype(jnp.int32), axis=1)


def shards(features, doc_labels, tree_perm, cluster_sizes):
    width = lax.axis_size("label")
    here = lax.axis_index("label")
    base = here * L_DEV
    slots = jnp.arange(L_DEV, dtype=jnp.int32)

    own_perm = lax.dynamic_slice_in_dim(tree_perm, base, L_DEV)
    incidence = jnp.sum(
        (doc_labels.T[:, None, :] == own_perm[None, :, None]).astype(jnp.float32), axis=0
    )
    partial_value = lax.dot_general(
        incidence,
        features,
        (((1,), (0,)), ((), ())),
        precision=lax.Precision.HIGHEST,
        preferred_element_type=jnp.float32,
    )
    groups = lax.axis_size("doc")
    depth = features.shape[1]
    pieces = lax.all_to_all(
        partial_value.reshape(groups, L_DEV // groups, depth), "doc", 0, 0, tiled=True
    )
    mine = unit_rows(jnp.sum(pieces, axis=0))
    label_rows = lax.all_to_all(
        jnp.broadcast_to(mine[None], (groups,) + mine.shape), "doc", 0, 0, tiled=True
    ).reshape(L_DEV, depth)

    starts = jnp.cumsum(cluster_sizes) - cluster_sizes
    cluster_ids = cluster_of(base + slots, starts)
    shard = jnp.arange(width, dtype=jnp.int32)
    first_id = cluster_of(shard * L_DEV, starts)
    last_id = cluster_of(shard * L_DEV + (L_DEV - 1), starts)

    same_cluster = (cluster_ids[:, None] == cluster_ids[None, :]).astype(jnp.float32)
    local_sum = jnp.dot(
        same_cluster,
        label_rows,
        precision=lax.Precision.HIGHEST,
        preferred_element_type=jnp.float32,
    )
    ends = jnp.stack([local_sum[0], local_sum[-1]])
    gathered = lax.all_to_all(
        jnp.broadcast_to(ends[None], (width,) + ends.shape), "label", 0, 0, tiled=True
    ).reshape(2 * width, -1)

    doc_unit = unit_rows(features)
    row_scores = lax.dot_general(
        doc_unit,
        label_rows,
        (((1,), (1,)), ((), ())),
        precision=lax.Precision.HIGHEST,
        preferred_element_type=jnp.float32,
    )
    other = (shard != here)[None, :]
    take_first = (first_id[None, :] == cluster_ids[:, None]) & other
    take_last = (last_id[None, :] == cluster_ids[:, None]) & (first_id != last_id)[None, :] & other
    weights = jnp.stack([take_first, take_last], axis=2).reshape(L_DEV, 2 * width)
    cluster_sum = local_sum + jnp.dot(
        weights.astype(jnp.float32),
        gathered,
        precision=lax.Precision.HIGHEST,
        preferred_element_type=jnp.float32,
    )
    centroid = unit_rows(cluster_sum)
    return lax.dot_general(
        doc_unit,
        centroid,
        (((1,), (1,)), ((), ())),
        precision=lax.Precision.HIGHEST,
        preferred_element_type=jnp.float32,
    ) + row_scores


def solution(mesh):
    in_specs = (P("doc", None), P("doc", None), P(), P())
    out_specs = P("doc", "label")
    return jax.shard_map(shards, mesh=mesh, in_specs=in_specs, out_specs=out_specs, check_vma=False)
```

```python
import jax
import jax.numpy as jnp
from jax import lax
from jax.sharding import PartitionSpec as P

L_DEV = 256


EPS = 1e-06


def unit_rows(matrix):
    return matrix * lax.rsqrt(jnp.sum(matrix * matrix, axis=1, keepdims=True) + EPS)


def cluster_of(positions, starts):
    return jnp.sum((starts[None, 1:] <= positions[:, None]).astype(jnp.int32), axis=1)


def shards(features, doc_labels, tree_perm, cluster_sizes):
    width = lax.axis_size("label")
    here = lax.axis_index("label")
    base = here * L_DEV
    slots = jnp.arange(L_DEV, dtype=jnp.int32)

    own_perm = lax.dynamic_slice_in_dim(tree_perm, base, L_DEV)
    incidence = jnp.sum(
        (doc_labels.T[:, None, :] == own_perm[None, :, None]).astype(jnp.float32), axis=0
    )
    partial_value = lax.dot_general(
        incidence,
        features,
        (((1,), (0,)), ((), ())),
        precision=lax.Precision.HIGHEST,
        preferred_element_type=jnp.float32,
    )
    groups = lax.axis_size("doc")
    depth = features.shape[1]
    pieces = lax.all_to_all(
        partial_value.reshape(groups, L_DEV // groups, depth), "doc", 0, 0, tiled=True
    )
    mine = unit_rows(jnp.sum(pieces, axis=0))
    label_rows = lax.all_to_all(
        jnp.broadcast_to(mine[None], (groups,) + mine.shape), "doc", 0, 0, tiled=True
    ).reshape(L_DEV, depth)

    starts = jnp.cumsum(cluster_sizes) - cluster_sizes
    cluster_ids = cluster_of(base + slots, starts)
    shard = jnp.arange(width, dtype=jnp.int32)
    first_id = cluster_of(shard * L_DEV, starts)
    last_id = cluster_of(shard * L_DEV + (L_DEV - 1), starts)

    same_cluster = (cluster_ids[:, None] == cluster_ids[None, :]).astype(jnp.float32)
    local_sum = jnp.dot(
        same_cluster,
        label_rows,
        precision=lax.Precision.HIGHEST,
        preferred_element_type=jnp.float32,
    )
    ends = jnp.stack([local_sum[0], local_sum[-1]])

    doc_unit = unit_rows(features)
    row_scores = lax.dot_general(
        doc_unit,
        label_rows,
        (((1,), (1,)), ((), ())),
        precision=lax.Precision.HIGHEST,
        preferred_element_type=jnp.float32,
    )

    lane = lax.axis_index("doc")
    my_first = first_id[here]
    my_last = last_id[here]
    extra = jnp.zeros_like(ends)
    for near in (1, groups + 1):
        for sign in (1, -1):
            pairs = []
            for i in range(groups):
                step = sign * (i + near)
                for j in range(width):
                    if 0 <= j + step < width:
                        pairs.append((i * width + j, i * width + j + step))
            got = lax.ppermute(ends, ("doc", "label"), pairs)
            source = here - sign * (lane + near)
            valid = (source >= 0) & (source < width)
            source = jnp.clip(source, 0, width - 1)
            src_first = first_id[source]
            src_last = last_id[source]
            parts = []
            for target in (my_first, my_last):
                part = jnp.where(
                    src_first == target, got[0], jnp.where(src_last == target, got[1], 0.0)
                )
                parts.append(jnp.where(valid, part, 0.0))
            extra = extra + jnp.stack(parts)
    extra = jnp.sum(
        lax.all_to_all(
            jnp.broadcast_to(extra[None], (groups,) + extra.shape), "doc", 0, 0, tiled=True
        ),
        axis=0,
    )
    in_first = (cluster_ids == my_first)[:, None]
    in_last = ((cluster_ids == my_last) & (my_last != my_first))[:, None]
    cluster_sum = local_sum + jnp.where(in_first, extra[0][None, :], 0.0)
    cluster_sum = cluster_sum + jnp.where(in_last, extra[1][None, :], 0.0)
    centroid = unit_rows(cluster_sum)
    return lax.dot_general(
        doc_unit,
        centroid,
        (((1,), (1,)), ((), ())),
        precision=lax.Precision.HIGHEST,
        preferred_element_type=jnp.float32,
    ) + row_scores


def solution(mesh):
    in_specs = (P("doc", None), P("doc", None), P(), P())
    out_specs = P("doc", "label")
    return jax.shard_map(shards, mesh=mesh, in_specs=in_specs, out_specs=out_specs, check_vma=False)
```

```python
import jax
import jax.numpy as jnp
from jax import lax
from jax.experimental import pallas as pl
from jax.experimental.pallas import tpu as pltpu
from jax.sharding import PartitionSpec as P

def split3(x):
    hi = x.astype(jnp.bfloat16)
    r1 = x - hi.astype(jnp.float32)
    mid = r1.astype(jnp.bfloat16)
    lo = (r1 - mid.astype(jnp.float32)).astype(jnp.bfloat16)
    return hi, mid, lo


def pifa_kernel(here_ref, perm_ref, lab_ref, feat_ref, out_ref):
    row = perm_ref[pl.ds(here_ref[0], 1), :]
    lab = lab_ref[...]
    inc_t = jnp.zeros((lab.shape[0], row.shape[1]), jnp.float32)
    for k in range(lab.shape[1]):
        inc_t = inc_t + (lab[:, k : k + 1] == row).astype(jnp.float32)
    inc = inc_t.T.astype(jnp.bfloat16)
    acc = None
    for piece in split3(feat_ref[...]):
        part = jnp.dot(inc, piece, preferred_element_type=jnp.float32)
        acc = part if acc is None else acc + part
    out_ref[...] = acc


def pifa_partial(here, perm_blocks, doc_labels, features):
    n_slots = perm_blocks.shape[1]
    return pl.pallas_call(
        pifa_kernel,
        out_shape=jax.ShapeDtypeStruct((n_slots, features.shape[1]), jnp.float32),
        in_specs=[
            pl.BlockSpec(memory_space=pltpu.SMEM),
            pl.BlockSpec(memory_space=pltpu.VMEM),
            pl.BlockSpec(memory_space=pltpu.VMEM),
            pl.BlockSpec(memory_space=pltpu.VMEM),
        ],
        out_specs=pl.BlockSpec(memory_space=pltpu.VMEM),
    )(here, perm_blocks, doc_labels, features)


L_DEV = 256


EPS = 1e-06


def unit_rows(matrix):
    return matrix * lax.rsqrt(jnp.sum(matrix * matrix, axis=1, keepdims=True) + EPS)


def cluster_of(positions, starts):
    return jnp.sum((starts[None, 1:] <= positions[:, None]).astype(jnp.int32), axis=1)


def shards(features, doc_labels, tree_perm, cluster_sizes):
    width = lax.axis_size("label")
    here = lax.axis_index("label")
    base = here * L_DEV
    slots = jnp.arange(L_DEV, dtype=jnp.int32)

    partial_value = pifa_partial(
        here.astype(jnp.int32)[None], tree_perm.reshape(width, L_DEV), doc_labels, features
    )
    groups = lax.axis_size("doc")
    depth = features.shape[1]
    pieces = lax.all_to_all(
        partial_value.reshape(groups, L_DEV // groups, depth), "doc", 0, 0, tiled=True
    )
    mine = unit_rows(jnp.sum(pieces, axis=0))
    label_rows = lax.all_to_all(
        jnp.broadcast_to(mine[None], (groups,) + mine.shape), "doc", 0, 0, tiled=True
    ).reshape(L_DEV, depth)

    starts = jnp.cumsum(cluster_sizes) - cluster_sizes
    cluster_ids = cluster_of(base + slots, starts)
    shard = jnp.arange(width, dtype=jnp.int32)
    first_id = cluster_of(shard * L_DEV, starts)
    last_id = cluster_of(shard * L_DEV + (L_DEV - 1), starts)

    same_cluster = (cluster_ids[:, None] == cluster_ids[None, :]).astype(jnp.float32)
    local_sum = jnp.dot(
        same_cluster,
        label_rows,
        precision=lax.Precision.HIGHEST,
        preferred_element_type=jnp.float32,
    )
    ends = jnp.stack([local_sum[0], local_sum[-1]])
    gathered = lax.all_to_all(
        jnp.broadcast_to(ends[None], (width,) + ends.shape), "label", 0, 0, tiled=True
    ).reshape(2 * width, -1)

    doc_unit = unit_rows(features)
    row_scores = lax.dot_general(
        doc_unit,
        label_rows,
        (((1,), (1,)), ((), ())),
        precision=lax.Precision.HIGHEST,
        preferred_element_type=jnp.float32,
    )
    other = (shard != here)[None, :]
    take_first = (first_id[None, :] == cluster_ids[:, None]) & other
    take_last = (last_id[None, :] == cluster_ids[:, None]) & (first_id != last_id)[None, :] & other
    weights = jnp.stack([take_first, take_last], axis=2).reshape(L_DEV, 2 * width)
    cluster_sum = local_sum + jnp.dot(
        weights.astype(jnp.float32),
        gathered,
        precision=lax.Precision.HIGHEST,
        preferred_element_type=jnp.float32,
    )
    centroid = unit_rows(cluster_sum)
    return lax.dot_general(
        doc_unit,
        centroid,
        (((1,), (1,)), ((), ())),
        precision=lax.Precision.HIGHEST,
        preferred_element_type=jnp.float32,
    ) + row_scores


def solution(mesh):
    in_specs = (P("doc", None), P("doc", None), P(), P())
    out_specs = P("doc", "label")
    return jax.shard_map(shards, mesh=mesh, in_specs=in_specs, out_specs=out_specs, check_vma=False)
```

```python
import jax
import jax.numpy as jnp
from jax import lax
from jax.experimental import pallas as pl
from jax.experimental.pallas import tpu as pltpu
from jax.sharding import PartitionSpec as P

def split3(x):
    hi = x.astype(jnp.bfloat16)
    r1 = x - hi.astype(jnp.float32)
    mid = r1.astype(jnp.bfloat16)
    lo = (r1 - mid.astype(jnp.float32)).astype(jnp.bfloat16)
    return hi, mid, lo


def pifa_kernel(perm_ref, lab_ref, feat_ref, out_ref):
    column = perm_ref[...]
    lab = lab_ref[...]
    inc = jnp.zeros((column.shape[0], lab.shape[1]), jnp.int32)
    for k in range(lab.shape[0]):
        inc = inc + (column == lab[k : k + 1, :]).astype(jnp.int32)
    inc = inc.astype(jnp.float32).astype(jnp.bfloat16)
    acc = None
    for piece in split3(feat_ref[...]):
        part = jnp.dot(inc, piece, preferred_element_type=jnp.float32)
        acc = part if acc is None else acc + part
    out_ref[...] = acc

def pifa_partial(own_perm, doc_labels, features):
    return pl.pallas_call(
        pifa_kernel,
        out_shape=jax.ShapeDtypeStruct((own_perm.shape[0], features.shape[1]), jnp.float32),
        in_specs=[pl.BlockSpec(memory_space=pltpu.VMEM)] * 3,
        out_specs=pl.BlockSpec(memory_space=pltpu.VMEM),
    )(own_perm[:, None], doc_labels.T, features)


L_DEV = 256


EPS = 1e-06


def unit_rows(matrix):
    return matrix * lax.rsqrt(jnp.sum(matrix * matrix, axis=1, keepdims=True) + EPS)


def cluster_of(positions, starts):
    return jnp.sum((starts[None, 1:] <= positions[:, None]).astype(jnp.int32), axis=1)


def shards(features, doc_labels, tree_perm, cluster_sizes):
    width = lax.axis_size("label")
    here = lax.axis_index("label")
    base = here * L_DEV
    slots = jnp.arange(L_DEV, dtype=jnp.int32)

    own_perm = lax.dynamic_slice_in_dim(tree_perm, base, L_DEV)
    partial_value = pifa_partial(own_perm, doc_labels, features)
    groups = lax.axis_size("doc")
    depth = features.shape[1]
    pieces = lax.all_to_all(
        partial_value.reshape(groups, L_DEV // groups, depth), "doc", 0, 0, tiled=True
    )
    mine = unit_rows(jnp.sum(pieces, axis=0))
    label_rows = lax.all_to_all(
        jnp.broadcast_to(mine[None], (groups,) + mine.shape), "doc", 0, 0, tiled=True
    ).reshape(L_DEV, depth)

    starts = jnp.cumsum(cluster_sizes) - cluster_sizes
    cluster_ids = cluster_of(base + slots, starts)
    shard = jnp.arange(width, dtype=jnp.int32)
    first_id = cluster_of(shard * L_DEV, starts)
    last_id = cluster_of(shard * L_DEV + (L_DEV - 1), starts)

    same_cluster = (cluster_ids[:, None] == cluster_ids[None, :]).astype(jnp.float32)
    local_sum = jnp.dot(
        same_cluster,
        label_rows,
        precision=lax.Precision.HIGHEST,
        preferred_element_type=jnp.float32,
    )
    ends = jnp.stack([local_sum[0], local_sum[-1]])
    gathered = lax.all_to_all(
        jnp.broadcast_to(ends[None], (width,) + ends.shape), "label", 0, 0, tiled=True
    ).reshape(2 * width, -1)

    doc_unit = unit_rows(features)
    row_scores = lax.dot_general(
        doc_unit,
        label_rows,
        (((1,), (1,)), ((), ())),
        precision=lax.Precision.HIGHEST,
        preferred_element_type=jnp.float32,
    )
    other = (shard != here)[None, :]
    take_first = (first_id[None, :] == cluster_ids[:, None]) & other
    take_last = (last_id[None, :] == cluster_ids[:, None]) & (first_id != last_id)[None, :] & other
    weights = jnp.stack([take_first, take_last], axis=2).reshape(L_DEV, 2 * width)
    cluster_sum = local_sum + jnp.dot(
        weights.astype(jnp.float32),
        gathered,
        precision=lax.Precision.HIGHEST,
        preferred_element_type=jnp.float32,
    )
    centroid = unit_rows(cluster_sum)
    return lax.dot_general(
        doc_unit,
        centroid,
        (((1,), (1,)), ((), ())),
        precision=lax.Precision.HIGHEST,
        preferred_element_type=jnp.float32,
    ) + row_scores


def solution(mesh):
    in_specs = (P("doc", None), P("doc", None), P(), P())
    out_specs = P("doc", "label")
    return jax.shard_map(shards, mesh=mesh, in_specs=in_specs, out_specs=out_specs, check_vma=False)
```

```python
import jax
import jax.numpy as jnp
from jax import lax
from jax.experimental import pallas as pl
from jax.experimental.pallas import tpu as pltpu
from jax.sharding import PartitionSpec as P

def split3(x):
    hi = x.astype(jnp.bfloat16)
    r1 = x - hi.astype(jnp.float32)
    mid = r1.astype(jnp.bfloat16)
    lo = (r1 - mid.astype(jnp.float32)).astype(jnp.bfloat16)
    return hi, mid, lo


def pifa_kernel(perm_ref, lab_ref, feat_ref, out_ref, inc_ref):
    @pl.when(pl.program_id(0) == 0)
    def _():
        column = perm_ref[...]
        lab = lab_ref[...]
        inc = jnp.zeros((column.shape[0], lab.shape[1]), jnp.int32)
        for k in range(lab.shape[0]):
            inc = inc + (column == lab[k : k + 1, :]).astype(jnp.int32)
        inc_ref[...] = inc.astype(jnp.float32).astype(jnp.bfloat16)

    inc = inc_ref[...]
    acc = None
    for piece in split3(feat_ref[...]):
        part = jnp.dot(inc, piece, preferred_element_type=jnp.float32)
        acc = part if acc is None else acc + part
    out_ref[...] = acc


def pifa_partial(own_perm, doc_labels, features, block=256):
    slots = own_perm.shape[0]
    docs, depth = features.shape
    return pl.pallas_call(
        pifa_kernel,
        out_shape=jax.ShapeDtypeStruct((slots, depth), jnp.float32),
        grid=(depth // block,),
        in_specs=[
            pl.BlockSpec((slots, 1), lambda c: (0, 0)),
            pl.BlockSpec((doc_labels.shape[1], docs), lambda c: (0, 0)),
            pl.BlockSpec((docs, block), lambda c: (0, c)),
        ],
        out_specs=pl.BlockSpec((slots, block), lambda c: (0, c)),
        scratch_shapes=[pltpu.VMEM((slots, docs), jnp.bfloat16)],
    )(own_perm[:, None], doc_labels.T, features)

L_DEV = 256


EPS = 1e-06


def unit_rows(matrix):
    return matrix * lax.rsqrt(jnp.sum(matrix * matrix, axis=1, keepdims=True) + EPS)


def cluster_of(positions, starts):
    return jnp.sum((starts[None, 1:] <= positions[:, None]).astype(jnp.int32), axis=1)


def shards(features, doc_labels, tree_perm, cluster_sizes):
    width = lax.axis_size("label")
    here = lax.axis_index("label")
    base = here * L_DEV
    slots = jnp.arange(L_DEV, dtype=jnp.int32)

    own_perm = lax.dynamic_slice_in_dim(tree_perm, base, L_DEV)
    partial_value = pifa_partial(own_perm, doc_labels, features)
    groups = lax.axis_size("doc")
    depth = features.shape[1]
    pieces = lax.all_to_all(
        partial_value.reshape(groups, L_DEV // groups, depth), "doc", 0, 0, tiled=True
    )
    mine = unit_rows(jnp.sum(pieces, axis=0))
    label_rows = lax.all_to_all(
        jnp.broadcast_to(mine[None], (groups,) + mine.shape), "doc", 0, 0, tiled=True
    ).reshape(L_DEV, depth)

    starts = jnp.cumsum(cluster_sizes) - cluster_sizes
    cluster_ids = cluster_of(base + slots, starts)
    shard = jnp.arange(width, dtype=jnp.int32)
    first_id = cluster_of(shard * L_DEV, starts)
    last_id = cluster_of(shard * L_DEV + (L_DEV - 1), starts)

    same_cluster = (cluster_ids[:, None] == cluster_ids[None, :]).astype(jnp.float32)
    local_sum = jnp.dot(
        same_cluster,
        label_rows,
        precision=lax.Precision.HIGHEST,
        preferred_element_type=jnp.float32,
    )
    ends = jnp.stack([local_sum[0], local_sum[-1]])
    gathered = lax.all_to_all(
        jnp.broadcast_to(ends[None], (width,) + ends.shape), "label", 0, 0, tiled=True
    ).reshape(2 * width, -1)

    doc_unit = unit_rows(features)
    row_scores = lax.dot_general(
        doc_unit,
        label_rows,
        (((1,), (1,)), ((), ())),
        precision=lax.Precision.HIGHEST,
        preferred_element_type=jnp.float32,
    )
    other = (shard != here)[None, :]
    take_first = (first_id[None, :] == cluster_ids[:, None]) & other
    take_last = (last_id[None, :] == cluster_ids[:, None]) & (first_id != last_id)[None, :] & other
    weights = jnp.stack([take_first, take_last], axis=2).reshape(L_DEV, 2 * width)
    cluster_sum = local_sum + jnp.dot(
        weights.astype(jnp.float32),
        gathered,
        precision=lax.Precision.HIGHEST,
        preferred_element_type=jnp.float32,
    )
    centroid = unit_rows(cluster_sum)
    return lax.dot_general(
        doc_unit,
        centroid,
        (((1,), (1,)), ((), ())),
        precision=lax.Precision.HIGHEST,
        preferred_element_type=jnp.float32,
    ) + row_scores


def solution(mesh):
    in_specs = (P("doc", None), P("doc", None), P(), P())
    out_specs = P("doc", "label")
    return jax.shard_map(shards, mesh=mesh, in_specs=in_specs, out_specs=out_specs, check_vma=False)
```

```python
import jax
import jax.numpy as jnp
from jax import lax
from jax.experimental import pallas as pl
from jax.experimental.pallas import tpu as pltpu
from jax.sharding import PartitionSpec as P

def split3(x):
    hi = x.astype(jnp.bfloat16)
    r1 = x - hi.astype(jnp.float32)
    mid = r1.astype(jnp.bfloat16)
    lo = (r1 - mid.astype(jnp.float32)).astype(jnp.bfloat16)
    return hi, mid, lo


def pifa_kernel(perm_ref, lab_ref, feat_ref, out_ref, inc_ref):
    @pl.when(pl.program_id(0) == 0)
    def _():
        column = perm_ref[...]
        lab = lab_ref[...]
        inc = jnp.zeros((column.shape[0], lab.shape[1]), jnp.int32)
        for k in range(lab.shape[0]):
            inc = inc + (column == lab[k : k + 1, :]).astype(jnp.int32)
        inc_ref[...] = inc.astype(jnp.float32).astype(jnp.bfloat16)

    inc = inc_ref[...]
    acc = None
    for piece in split3(feat_ref[...]):
        part = jnp.dot(inc, piece, preferred_element_type=jnp.float32)
        acc = part if acc is None else acc + part
    out_ref[...] = acc


def pifa_partial(own_perm, doc_labels, features, block=256):
    slots = own_perm.shape[0]
    docs, depth = features.shape
    return pl.pallas_call(
        pifa_kernel,
        out_shape=jax.ShapeDtypeStruct((slots, depth), jnp.float32),
        grid=(depth // block,),
        in_specs=[
            pl.BlockSpec((slots, 1), lambda c: (0, 0)),
            pl.BlockSpec((doc_labels.shape[1], docs), lambda c: (0, 0)),
            pl.BlockSpec((docs, block), lambda c: (0, c)),
        ],
        out_specs=pl.BlockSpec((slots, block), lambda c: (0, c)),
        scratch_shapes=[pltpu.VMEM((slots, docs), jnp.bfloat16)],
    )(own_perm[:, None], doc_labels.T, features)

L_DEV = 256


EPS = 1e-06


def unit_rows(matrix):
    return matrix * lax.rsqrt(jnp.sum(matrix * matrix, axis=1, keepdims=True) + EPS)


def cluster_of(positions, starts):
    return jnp.sum((starts[None, 1:] <= positions[:, None]).astype(jnp.int32), axis=1)


def shards(features, doc_labels, tree_perm, cluster_sizes):
    width = lax.axis_size("label")
    here = lax.axis_index("label")
    base = here * L_DEV
    slots = jnp.arange(L_DEV, dtype=jnp.int32)

    own_perm = lax.dynamic_slice_in_dim(tree_perm, base, L_DEV)
    partial_value = pifa_partial(own_perm, doc_labels, features)
    groups = lax.axis_size("doc")
    depth = features.shape[1]
    pieces = lax.all_to_all(
        partial_value.reshape(groups, L_DEV // groups, depth), "doc", 0, 0, tiled=True
    )
    mine = unit_rows(jnp.sum(pieces, axis=0))
    label_rows = lax.all_to_all(
        jnp.broadcast_to(mine[None], (groups,) + mine.shape), "doc", 0, 0, tiled=True
    ).reshape(L_DEV, depth)

    starts = jnp.cumsum(cluster_sizes) - cluster_sizes
    cluster_ids = cluster_of(base + slots, starts)
    shard = jnp.arange(width, dtype=jnp.int32)
    first_id = cluster_of(shard * L_DEV, starts)
    last_id = cluster_of(shard * L_DEV + (L_DEV - 1), starts)

    same_cluster = (cluster_ids[:, None] == cluster_ids[None, :]).astype(jnp.float32)
    local_sum = jnp.dot(
        same_cluster,
        label_rows,
        precision=lax.Precision.HIGHEST,
        preferred_element_type=jnp.float32,
    )
    ends = jnp.stack([local_sum[0], local_sum[-1]])
    gathered = lax.all_to_all(
        jnp.broadcast_to(ends[None], (width,) + ends.shape), "label", 0, 0, tiled=True
    ).reshape(2 * width, -1)

    other = (shard != here)[None, :]
    take_first = (first_id[None, :] == cluster_ids[:, None]) & other
    take_last = (last_id[None, :] == cluster_ids[:, None]) & (first_id != last_id)[None, :] & other
    weights = jnp.stack([take_first, take_last], axis=2).reshape(L_DEV, 2 * width)
    doc_unit = unit_rows(features)
    both = lax.dot_general(
        doc_unit,
        jnp.concatenate([label_rows, local_sum]),
        (((1,), (1,)), ((), ())),
        precision=lax.Precision.HIGHEST,
        preferred_element_type=jnp.float32,
    )
    row_scores = both[:, :L_DEV]
    near_scores = both[:, L_DEV:]
    weights = weights.astype(jnp.float32)
    cluster_sum = local_sum + jnp.dot(
        weights, gathered, precision=lax.Precision.HIGHEST, preferred_element_type=jnp.float32
    )
    scale = lax.rsqrt(jnp.sum(cluster_sum * cluster_sum, axis=1) + EPS)
    far_scores = jnp.dot(
        lax.dot_general(
            doc_unit,
            gathered,
            (((1,), (1,)), ((), ())),
            precision=lax.Precision.HIGHEST,
            preferred_element_type=jnp.float32,
        ),
        weights.T,
        precision=lax.Precision.HIGHEST,
        preferred_element_type=jnp.float32,
    )
    return row_scores + (near_scores + far_scores) * scale[None, :]


def solution(mesh):
    in_specs = (P("doc", None), P("doc", None), P(), P())
    out_specs = P("doc", "label")
    return jax.shard_map(shards, mesh=mesh, in_specs=in_specs, out_specs=out_specs, check_vma=False)
```

```python
import jax
import jax.numpy as jnp
from jax import lax
from jax.experimental import pallas as pl
from jax.experimental.pallas import tpu as pltpu
from jax.sharding import PartitionSpec as P

def split3(x):
    hi = x.astype(jnp.bfloat16)
    r1 = x - hi.astype(jnp.float32)
    mid = r1.astype(jnp.bfloat16)
    lo = (r1 - mid.astype(jnp.float32)).astype(jnp.bfloat16)
    return hi, mid, lo


def pifa_kernel(perm_ref, lab_ref, feat_ref, out_ref):
    column = perm_ref[...]
    lab = lab_ref[...]
    inc = jnp.zeros((column.shape[0], lab.shape[1]), jnp.int32)
    for k in range(lab.shape[0]):
        inc = inc + (column == lab[k : k + 1, :]).astype(jnp.int32)
    inc = inc.astype(jnp.float32).astype(jnp.bfloat16)
    acc = None
    for piece in split3(feat_ref[...]):
        part = jnp.dot(inc, piece, preferred_element_type=jnp.float32)
        acc = part if acc is None else acc + part
    out_ref[...] = acc

def pifa_partial(own_perm, doc_labels, features):
    return pl.pallas_call(
        pifa_kernel,
        out_shape=jax.ShapeDtypeStruct((own_perm.shape[0], features.shape[1]), jnp.float32),
        in_specs=[pl.BlockSpec(memory_space=pltpu.VMEM)] * 3,
        out_specs=pl.BlockSpec(memory_space=pltpu.VMEM),
    )(own_perm[:, None], doc_labels.T, features)


L_DEV = 256


EPS = 1e-06


def unit_rows(matrix):
    return matrix * lax.rsqrt(jnp.sum(matrix * matrix, axis=1, keepdims=True) + EPS)


def cluster_of(positions, starts):
    return jnp.sum((starts[None, 1:] <= positions[:, None]).astype(jnp.int32), axis=1)


def shards(features, doc_labels, tree_perm, cluster_sizes):
    width = lax.axis_size("label")
    here = lax.axis_index("label")
    base = here * L_DEV
    slots = jnp.arange(L_DEV, dtype=jnp.int32)

    own_perm = lax.dynamic_slice_in_dim(tree_perm, base, L_DEV)
    partial_value = pifa_partial(own_perm, doc_labels, features)
    groups = lax.axis_size("doc")
    depth = features.shape[1]
    pieces = lax.all_to_all(
        partial_value.reshape(groups, L_DEV // groups, depth), "doc", 0, 0, tiled=True
    )
    mine = unit_rows(jnp.sum(pieces, axis=0))
    label_rows = lax.all_gather(mine, "doc", tiled=True)

    starts = jnp.cumsum(cluster_sizes) - cluster_sizes
    cluster_ids = cluster_of(base + slots, starts)
    shard = jnp.arange(width, dtype=jnp.int32)
    first_id = cluster_of(shard * L_DEV, starts)
    last_id = cluster_of(shard * L_DEV + (L_DEV - 1), starts)
    my_first = first_id[here]
    my_last = last_id[here]

    chunk = L_DEV // groups
    chunk_ids = cluster_of(base + lax.axis_index("doc") * chunk + jnp.arange(chunk), starts)
    ends = jnp.stack(
        [
            jnp.sum(jnp.where((chunk_ids == my_first)[:, None], mine, 0.0), axis=0),
            jnp.sum(jnp.where((chunk_ids == my_last)[:, None], mine, 0.0), axis=0),
        ]
    )
    gathered = lax.all_to_all(
        jnp.broadcast_to(ends[None], (width,) + ends.shape), "label", 0, 0, tiled=True
    )
    other = shard != here
    parts = []
    for target in (my_first, my_last):
        use_first = (first_id == target) & other
        use_last = (last_id == target) & (first_id != last_id) & other
        parts.append(
            jnp.sum(
                jnp.where(use_first[:, None], gathered[:, 0], 0.0)
                + jnp.where(use_last[:, None], gathered[:, 1], 0.0),
                axis=0,
            )
        )
    extra = jnp.stack(parts)
    extra = jnp.sum(
        lax.all_to_all(
            jnp.broadcast_to(extra[None], (groups,) + extra.shape), "doc", 0, 0, tiled=True
        ),
        axis=0,
    )

    same_cluster = (cluster_ids[:, None] == cluster_ids[None, :]).astype(jnp.float32)
    local_sum = jnp.dot(
        same_cluster,
        label_rows,
        precision=lax.Precision.HIGHEST,
        preferred_element_type=jnp.float32,
    )
    doc_unit = unit_rows(features)
    row_scores = lax.dot_general(
        doc_unit,
        label_rows,
        (((1,), (1,)), ((), ())),
        precision=lax.Precision.HIGHEST,
        preferred_element_type=jnp.float32,
    )
    in_first = (cluster_ids == my_first)[:, None]
    in_last = ((cluster_ids == my_last) & (my_last != my_first))[:, None]
    cluster_sum = local_sum + jnp.where(in_first, extra[0][None, :], 0.0)
    cluster_sum = cluster_sum + jnp.where(in_last, extra[1][None, :], 0.0)
    centroid = unit_rows(cluster_sum)
    return lax.dot_general(
        doc_unit,
        centroid,
        (((1,), (1,)), ((), ())),
        precision=lax.Precision.HIGHEST,
        preferred_element_type=jnp.float32,
    ) + row_scores


def solution(mesh):
    in_specs = (P("doc", None), P("doc", None), P(), P())
    out_specs = P("doc", "label")
    return jax.shard_map(shards, mesh=mesh, in_specs=in_specs, out_specs=out_specs, check_vma=False)
```

```python
import jax
import jax.numpy as jnp
from jax import lax
from jax.experimental import pallas as pl
from jax.experimental.pallas import tpu as pltpu
from jax.sharding import PartitionSpec as P

def split3(x):
    hi = x.astype(jnp.bfloat16)
    r1 = x - hi.astype(jnp.float32)
    mid = r1.astype(jnp.bfloat16)
    lo = (r1 - mid.astype(jnp.float32)).astype(jnp.bfloat16)
    return hi, mid, lo


def pifa_kernel(perm_ref, lab_ref, feat_ref, out_ref):
    column = perm_ref[...]
    lab = lab_ref[...]
    inc = jnp.zeros((column.shape[0], lab.shape[1]), jnp.int32)
    for k in range(lab.shape[0]):
        inc = inc + (column == lab[k : k + 1, :]).astype(jnp.int32)
    inc = inc.astype(jnp.float32).astype(jnp.bfloat16)
    acc = None
    for piece in split3(feat_ref[...]):
        part = jnp.dot(inc, piece, preferred_element_type=jnp.float32)
        acc = part if acc is None else acc + part
    out_ref[...] = acc

def pifa_partial(own_perm, doc_labels, features):
    return pl.pallas_call(
        pifa_kernel,
        out_shape=jax.ShapeDtypeStruct((own_perm.shape[0], features.shape[1]), jnp.float32),
        in_specs=[pl.BlockSpec(memory_space=pltpu.VMEM)] * 3,
        out_specs=pl.BlockSpec(memory_space=pltpu.VMEM),
    )(own_perm[:, None], doc_labels.T, features)


L_DEV = 256


EPS = 1e-06


def unit_rows(matrix):
    return matrix * lax.rsqrt(jnp.sum(matrix * matrix, axis=1, keepdims=True) + EPS)


def cluster_of(positions, starts):
    return jnp.sum((starts[None, 1:] <= positions[:, None]).astype(jnp.int32), axis=1)


def shards(features, doc_labels, tree_perm, cluster_sizes):
    width = lax.axis_size("label")
    here = lax.axis_index("label")
    base = here * L_DEV
    slots = jnp.arange(L_DEV, dtype=jnp.int32)

    own_perm = lax.dynamic_slice_in_dim(tree_perm, base, L_DEV)
    partial_value = pifa_partial(own_perm, doc_labels, features)
    groups = lax.axis_size("doc")
    depth = features.shape[1]
    pieces = lax.all_to_all(
        partial_value.reshape(groups, L_DEV // groups, depth), "doc", 0, 0, tiled=True
    )
    mine = unit_rows(jnp.sum(pieces, axis=0))
    label_rows = lax.all_to_all(
        jnp.broadcast_to(mine[None], (groups,) + mine.shape), "doc", 0, 0, tiled=True
    ).reshape(L_DEV, depth)

    starts = jnp.cumsum(cluster_sizes) - cluster_sizes
    cluster_ids = cluster_of(base + slots, starts)
    shard = jnp.arange(width, dtype=jnp.int32)
    first_id = cluster_of(shard * L_DEV, starts)
    last_id = cluster_of(shard * L_DEV + (L_DEV - 1), starts)

    same_cluster = (cluster_ids[:, None] == cluster_ids[None, :]).astype(jnp.float32)
    local_sum = jnp.dot(
        same_cluster,
        label_rows,
        precision=lax.Precision.HIGH,
        preferred_element_type=jnp.float32,
    )
    ends = jnp.stack([local_sum[0], local_sum[-1]])
    gathered = lax.all_to_all(
        jnp.broadcast_to(ends[None], (width,) + ends.shape), "label", 0, 0, tiled=True
    ).reshape(2 * width, -1)

    doc_unit = unit_rows(features)
    row_scores = lax.dot_general(
        doc_unit,
        label_rows,
        (((1,), (1,)), ((), ())),
        precision=lax.Precision.HIGH,
        preferred_element_type=jnp.float32,
    )
    other = (shard != here)[None, :]
    take_first = (first_id[None, :] == cluster_ids[:, None]) & other
    take_last = (last_id[None, :] == cluster_ids[:, None]) & (first_id != last_id)[None, :] & other
    weights = jnp.stack([take_first, take_last], axis=2).reshape(L_DEV, 2 * width)
    cluster_sum = local_sum + jnp.dot(
        weights.astype(jnp.float32),
        gathered,
        precision=lax.Precision.HIGH,
        preferred_element_type=jnp.float32,
    )
    centroid = unit_rows(cluster_sum)
    return lax.dot_general(
        doc_unit,
        centroid,
        (((1,), (1,)), ((), ())),
        precision=lax.Precision.HIGH,
        preferred_element_type=jnp.float32,
    ) + row_scores


def solution(mesh):
    in_specs = (P("doc", None), P("doc", None), P(), P())
    out_specs = P("doc", "label")
    return jax.shard_map(shards, mesh=mesh, in_specs=in_specs, out_specs=out_specs, check_vma=False)
```

```python
import jax
import jax.numpy as jnp
from jax import lax
from jax.experimental import pallas as pl
from jax.experimental.pallas import tpu as pltpu
from jax.sharding import PartitionSpec as P

def split3(x):
    hi = x.astype(jnp.bfloat16)
    r1 = x - hi.astype(jnp.float32)
    mid = r1.astype(jnp.bfloat16)
    lo = (r1 - mid.astype(jnp.float32)).astype(jnp.bfloat16)
    return hi, mid, lo


def pifa_kernel(perm_ref, lab_ref, feat_ref, out_ref):
    column = perm_ref[...]
    lab = lab_ref[...]
    inc = jnp.zeros((column.shape[0], lab.shape[1]), jnp.int32)
    for k in range(lab.shape[0]):
        inc = inc + (column == lab[k : k + 1, :]).astype(jnp.int32)
    inc = inc.astype(jnp.float32).astype(jnp.bfloat16)
    acc = None
    for piece in split3(feat_ref[...]):
        part = jnp.dot(inc, piece, preferred_element_type=jnp.float32)
        acc = part if acc is None else acc + part
    out_ref[...] = acc

def pifa_partial(own_perm, doc_labels, features):
    return pl.pallas_call(
        pifa_kernel,
        out_shape=jax.ShapeDtypeStruct((own_perm.shape[0], features.shape[1]), jnp.float32),
        in_specs=[pl.BlockSpec(memory_space=pltpu.VMEM)] * 3,
        out_specs=pl.BlockSpec(memory_space=pltpu.VMEM),
    )(own_perm[:, None], doc_labels.T, features)


L_DEV = 256


EPS = 1e-06


def unit_rows(matrix):
    return matrix * lax.rsqrt(jnp.sum(matrix * matrix, axis=1, keepdims=True) + EPS)


def cluster_of(positions, starts):
    return jnp.sum((starts[None, 1:] <= positions[:, None]).astype(jnp.int32), axis=1)


def shards(features, doc_labels, tree_perm, cluster_sizes):
    width = lax.axis_size("label")
    here = lax.axis_index("label")
    base = here * L_DEV
    slots = jnp.arange(L_DEV, dtype=jnp.int32)

    own_perm = lax.dynamic_slice_in_dim(tree_perm, base, L_DEV)
    partial_value = pifa_partial(own_perm, doc_labels, features)
    groups = lax.axis_size("doc")
    depth = features.shape[1]
    pieces = lax.all_to_all(
        partial_value.reshape(groups, L_DEV // groups, depth), "doc", 0, 0, tiled=True
    )
    mine = unit_rows(jnp.sum(pieces, axis=0))
    label_rows = lax.all_to_all(
        jnp.broadcast_to(mine[None], (groups,) + mine.shape), "doc", 0, 0, tiled=True
    ).reshape(L_DEV, depth)

    starts = jnp.cumsum(cluster_sizes) - cluster_sizes
    cluster_ids = cluster_of(base + slots, starts)
    shard = jnp.arange(width, dtype=jnp.int32)
    first_id = cluster_of(shard * L_DEV, starts)
    last_id = cluster_of(shard * L_DEV + (L_DEV - 1), starts)

    same_cluster = (cluster_ids[:, None] == cluster_ids[None, :]).astype(jnp.float32)
    local_sum = jnp.dot(
        same_cluster,
        label_rows,
        precision=lax.Precision.HIGH,
        preferred_element_type=jnp.float32,
    )
    above = shard > here
    sending = jnp.where(above[:, None], local_sum[-1][None, :], local_sum[0][None, :])
    gathered = lax.all_to_all(sending, "label", 0, 0, tiled=True)

    doc_unit = unit_rows(features)
    row_scores = lax.dot_general(
        doc_unit,
        label_rows,
        (((1,), (1,)), ((), ())),
        precision=lax.Precision.HIGH,
        preferred_element_type=jnp.float32,
    )
    below = shard < here
    take_below = (last_id[None, :] == cluster_ids[:, None]) & below[None, :]
    take_above = (first_id[None, :] == cluster_ids[:, None]) & above[None, :]
    weights = take_below | take_above
    cluster_sum = local_sum + jnp.dot(
        weights.astype(jnp.float32),
        gathered,
        precision=lax.Precision.HIGH,
        preferred_element_type=jnp.float32,
    )
    centroid = unit_rows(cluster_sum)
    return lax.dot_general(
        doc_unit,
        centroid,
        (((1,), (1,)), ((), ())),
        precision=lax.Precision.HIGH,
        preferred_element_type=jnp.float32,
    ) + row_scores


def solution(mesh):
    in_specs = (P("doc", None), P("doc", None), P(), P())
    out_specs = P("doc", "label")
    return jax.shard_map(shards, mesh=mesh, in_specs=in_specs, out_specs=out_specs, check_vma=False)
```

```python
import jax
import jax.numpy as jnp
from jax import lax
from jax.sharding import PartitionSpec as P

L_DEV = 256


EPS = 1e-06


def unit_rows(matrix):
    return matrix * lax.rsqrt(jnp.sum(matrix * matrix, axis=1, keepdims=True) + EPS)


def cluster_of(positions, starts):
    return jnp.sum((starts[None, 1:] <= positions[:, None]).astype(jnp.int32), axis=1)


def shards(features, doc_labels, tree_perm, cluster_sizes):
    width = lax.axis_size("label")
    here = lax.axis_index("label")
    base = here * L_DEV
    slots = jnp.arange(L_DEV, dtype=jnp.int32)

    own_perm = lax.dynamic_slice_in_dim(tree_perm, base, L_DEV)
    incidence = jnp.sum(
        (doc_labels.T[:, None, :] == own_perm[None, :, None]).astype(jnp.float32), axis=0
    )
    partial_value = jnp.dot(
        incidence, features, precision=lax.Precision.HIGH, preferred_element_type=jnp.float32
    )
    groups = lax.axis_size("doc")
    depth = features.shape[1]
    pieces = lax.all_to_all(
        partial_value.reshape(groups, L_DEV // groups, depth), "doc", 0, 0, tiled=True
    )
    mine = unit_rows(jnp.sum(pieces, axis=0))
    label_rows = lax.all_to_all(
        jnp.broadcast_to(mine[None], (groups,) + mine.shape), "doc", 0, 0, tiled=True
    ).reshape(L_DEV, depth)

    starts = jnp.cumsum(cluster_sizes) - cluster_sizes
    cluster_ids = cluster_of(base + slots, starts)
    shard = jnp.arange(width, dtype=jnp.int32)
    first_id = cluster_of(shard * L_DEV, starts)
    last_id = cluster_of(shard * L_DEV + (L_DEV - 1), starts)

    same_cluster = (cluster_ids[:, None] == cluster_ids[None, :]).astype(jnp.float32)
    local_sum = jnp.dot(
        same_cluster,
        label_rows,
        precision=lax.Precision.HIGH,
        preferred_element_type=jnp.float32,
    )
    above = shard > here
    sending = jnp.where(above[:, None], local_sum[-1][None, :], local_sum[0][None, :])
    gathered = lax.all_to_all(sending, "label", 0, 0, tiled=True)

    doc_unit = unit_rows(features)
    row_scores = lax.dot_general(
        doc_unit,
        label_rows,
        (((1,), (1,)), ((), ())),
        precision=lax.Precision.HIGH,
        preferred_element_type=jnp.float32,
    )
    below = shard < here
    take_below = (last_id[None, :] == cluster_ids[:, None]) & below[None, :]
    take_above = (first_id[None, :] == cluster_ids[:, None]) & above[None, :]
    weights = take_below | take_above
    cluster_sum = local_sum + jnp.dot(
        weights.astype(jnp.float32),
        gathered,
        precision=lax.Precision.HIGH,
        preferred_element_type=jnp.float32,
    )
    centroid = unit_rows(cluster_sum)
    return lax.dot_general(
        doc_unit,
        centroid,
        (((1,), (1,)), ((), ())),
        precision=lax.Precision.HIGH,
        preferred_element_type=jnp.float32,
    ) + row_scores


def solution(mesh):
    in_specs = (P("doc", None), P("doc", None), P(), P())
    out_specs = P("doc", "label")
    return jax.shard_map(shards, mesh=mesh, in_specs=in_specs, out_specs=out_specs, check_vma=False)
```

```python
import jax
import jax.numpy as jnp
from jax import lax
from jax.sharding import PartitionSpec as P

L_DEV = 256


EPS = 1e-06


def unit_rows(matrix):
    return matrix * lax.rsqrt(jnp.sum(matrix * matrix, axis=1, keepdims=True) + EPS)


def cluster_of(positions, starts):
    return jnp.sum((starts[None, 1:] <= positions[:, None]).astype(jnp.int32), axis=1)


def shards(features, doc_labels, tree_perm, cluster_sizes):
    width = lax.axis_size("label")
    here = lax.axis_index("label")
    base = here * L_DEV
    slots = jnp.arange(L_DEV, dtype=jnp.int32)

    own_perm = lax.dynamic_slice_in_dim(tree_perm, base, L_DEV)
    incidence = jnp.sum(
        (doc_labels.T[:, None, :] == own_perm[None, :, None]).astype(jnp.float32), axis=0
    )
    partial_value = jnp.dot(
        incidence, features, precision=lax.Precision.HIGH, preferred_element_type=jnp.float32
    )
    groups = lax.axis_size("doc")
    depth = features.shape[1]
    pieces = lax.all_to_all(
        partial_value.reshape(groups, L_DEV // groups, depth), "doc", 0, 0, tiled=True
    )
    mine = unit_rows(jnp.sum(pieces, axis=0))
    label_rows = lax.all_to_all(
        jnp.broadcast_to(mine[None], (groups,) + mine.shape), "doc", 0, 0, tiled=True
    ).reshape(L_DEV, depth)

    starts = jnp.cumsum(cluster_sizes) - cluster_sizes
    cluster_ids = cluster_of(base + slots, starts)
    shard = jnp.arange(width, dtype=jnp.int32)
    first_id = cluster_of(shard * L_DEV, starts)
    last_id = cluster_of(shard * L_DEV + (L_DEV - 1), starts)

    same_cluster = (cluster_ids[:, None] == cluster_ids[None, :]).astype(jnp.float32)
    local_sum = jnp.dot(
        same_cluster,
        label_rows,
        precision=lax.Precision.HIGH,
        preferred_element_type=jnp.float32,
    )
    above = shard > here
    first_sum = jnp.sum(jnp.where((cluster_ids == first_id[here])[:, None], label_rows, 0.0), axis=0)
    last_sum = jnp.sum(jnp.where((cluster_ids == last_id[here])[:, None], label_rows, 0.0), axis=0)
    sending = jnp.where(above[:, None], last_sum[None, :], first_sum[None, :])
    gathered = lax.all_to_all(sending, "label", 0, 0, tiled=True)

    doc_unit = unit_rows(features)
    row_scores = lax.dot_general(
        doc_unit,
        label_rows,
        (((1,), (1,)), ((), ())),
        precision=lax.Precision.HIGH,
        preferred_element_type=jnp.float32,
    )
    below = shard < here
    take_below = (last_id[None, :] == cluster_ids[:, None]) & below[None, :]
    take_above = (first_id[None, :] == cluster_ids[:, None]) & above[None, :]
    weights = take_below | take_above
    cluster_sum = local_sum + jnp.dot(
        weights.astype(jnp.float32),
        gathered,
        precision=lax.Precision.HIGH,
        preferred_element_type=jnp.float32,
    )
    centroid = unit_rows(cluster_sum)
    return lax.dot_general(
        doc_unit,
        centroid,
        (((1,), (1,)), ((), ())),
        precision=lax.Precision.HIGH,
        preferred_element_type=jnp.float32,
    ) + row_scores


def solution(mesh):
    in_specs = (P("doc", None), P("doc", None), P(), P())
    out_specs = P("doc", "label")
    return jax.shard_map(shards, mesh=mesh, in_specs=in_specs, out_specs=out_specs, check_vma=False)
```

```python
import jax
import jax.numpy as jnp
from jax import lax
from jax.sharding import Mesh, PartitionSpec as P

L_DEV = 256


EPS = 1e-06


def unit_rows(matrix):
    return matrix * lax.rsqrt(jnp.sum(matrix * matrix, axis=1, keepdims=True) + EPS)


def cluster_of(positions, starts):
    return jnp.sum((starts[None, 1:] <= positions[:, None]).astype(jnp.int32), axis=1)


def shards(features, doc_labels, tree_perm, cluster_sizes):
    width = lax.axis_size("label")
    here = lax.axis_index("label")
    base = here * L_DEV
    slots = jnp.arange(L_DEV, dtype=jnp.int32)

    own_perm = lax.dynamic_slice_in_dim(tree_perm, base, L_DEV)
    incidence = jnp.sum(
        (doc_labels.T[:, None, :] == own_perm[None, :, None]).astype(jnp.float32), axis=0
    )
    partial_value = jnp.dot(
        incidence, features, precision=lax.Precision.HIGH, preferred_element_type=jnp.float32
    )
    chips = lax.axis_size("dy")
    depth = features.shape[1]
    half = L_DEV // 2
    core = lax.axis_index("dc")
    sibling = [(0, 1), (1, 0)]
    halves = partial_value.reshape(2, half, depth)
    keep = jnp.where(core == 0, halves[0], halves[1])
    give = jnp.where(core == 0, halves[1], halves[0])
    chip_half = keep + lax.ppermute(give, "dc", sibling)
    pieces = lax.all_to_all(
        chip_half.reshape(chips, half // chips, depth), "dy", 0, 0, tiled=True
    )
    mine = unit_rows(jnp.sum(pieces, axis=0))
    own_half = lax.all_to_all(
        jnp.broadcast_to(mine[None], (chips,) + mine.shape), "dy", 0, 0, tiled=True
    ).reshape(half, depth)
    other_half = lax.ppermute(own_half, "dc", sibling)
    label_rows = jnp.where(
        core == 0,
        jnp.concatenate([own_half, other_half]),
        jnp.concatenate([other_half, own_half]),
    )

    starts = jnp.cumsum(cluster_sizes) - cluster_sizes
    cluster_ids = cluster_of(base + slots, starts)
    shard = jnp.arange(width, dtype=jnp.int32)
    first_id = cluster_of(shard * L_DEV, starts)
    last_id = cluster_of(shard * L_DEV + (L_DEV - 1), starts)

    same_cluster = (cluster_ids[:, None] == cluster_ids[None, :]).astype(jnp.float32)
    local_sum = jnp.dot(
        same_cluster,
        label_rows,
        precision=lax.Precision.HIGH,
        preferred_element_type=jnp.float32,
    )
    above = shard > here
    first_sum = jnp.sum(jnp.where((cluster_ids == first_id[here])[:, None], label_rows, 0.0), axis=0)
    last_sum = jnp.sum(jnp.where((cluster_ids == last_id[here])[:, None], label_rows, 0.0), axis=0)
    sending = jnp.where(above[:, None], last_sum[None, :], first_sum[None, :])
    gathered = lax.all_to_all(sending, "label", 0, 0, tiled=True)

    doc_unit = unit_rows(features)
    row_scores = lax.dot_general(
        doc_unit,
        label_rows,
        (((1,), (1,)), ((), ())),
        precision=lax.Precision.HIGH,
        preferred_element_type=jnp.float32,
    )
    below = shard < here
    take_below = (last_id[None, :] == cluster_ids[:, None]) & below[None, :]
    take_above = (first_id[None, :] == cluster_ids[:, None]) & above[None, :]
    weights = take_below | take_above
    cluster_sum = local_sum + jnp.dot(
        weights.astype(jnp.float32),
        gathered,
        precision=lax.Precision.HIGH,
        preferred_element_type=jnp.float32,
    )
    centroid = unit_rows(cluster_sum)
    return lax.dot_general(
        doc_unit,
        centroid,
        (((1,), (1,)), ((), ())),
        precision=lax.Precision.HIGH,
        preferred_element_type=jnp.float32,
    ) + row_scores


def solution(mesh):
    doc = mesh.shape["doc"]
    split = Mesh(mesh.devices.reshape(doc // 2, 2, -1), ("dy", "dc", "label"))
    docs = ("dy", "dc")
    in_specs = (P(docs, None), P(docs, None), P(), P())
    out_specs = P(docs, "label")
    return jax.shard_map(shards, mesh=split, in_specs=in_specs, out_specs=out_specs, check_vma=False)
```

```python
import jax
import jax.numpy as jnp
from jax import lax
from jax.sharding import Mesh, PartitionSpec as P

L_DEV = 256


EPS = 1e-06


def unit_rows(matrix):
    return matrix * lax.rsqrt(jnp.sum(matrix * matrix, axis=1, keepdims=True) + EPS)


def cluster_of(positions, starts):
    return jnp.sum((starts[None, 1:] <= positions[:, None]).astype(jnp.int32), axis=1)


def shards(features, doc_labels, tree_perm, cluster_sizes):
    width = lax.axis_size("label")
    here = lax.axis_index("label")
    base = here * L_DEV
    slots = jnp.arange(L_DEV, dtype=jnp.int32)

    own_perm = lax.dynamic_slice_in_dim(tree_perm, base, L_DEV)
    incidence = jnp.sum(
        (doc_labels.T[:, None, :] == own_perm[None, :, None]).astype(jnp.float32), axis=0
    )
    partial_value = jnp.dot(
        incidence, features, precision=lax.Precision.HIGH, preferred_element_type=jnp.float32
    )
    chips = lax.axis_size("dy")
    depth = features.shape[1]
    half = L_DEV // 2
    core = lax.axis_index("dc")
    sibling = [(0, 1), (1, 0)]
    halves = partial_value.reshape(2, half, depth)
    keep = jnp.where(core == 0, halves[0], halves[1])
    give = jnp.where(core == 0, halves[1], halves[0])
    chip_half = keep + lax.ppermute(give, "dc", sibling)
    pieces = lax.all_to_all(
        chip_half.reshape(chips, half // chips, depth), "dy", 0, 0, tiled=True
    )
    mine = unit_rows(jnp.sum(pieces, axis=0))
    own_half = lax.all_to_all(
        jnp.broadcast_to(mine[None], (chips,) + mine.shape), "dy", 0, 0, tiled=True
    ).reshape(half, depth)
    other_half = lax.ppermute(own_half, "dc", sibling)
    label_rows = jnp.where(
        core == 0,
        jnp.concatenate([own_half, other_half]),
        jnp.concatenate([other_half, own_half]),
    )

    starts = jnp.cumsum(cluster_sizes) - cluster_sizes
    cluster_ids = cluster_of(base + slots, starts)
    shard = jnp.arange(width, dtype=jnp.int32)
    first_id = cluster_of(shard * L_DEV, starts)
    last_id = cluster_of(shard * L_DEV + (L_DEV - 1), starts)

    same_cluster = (cluster_ids[:, None] == cluster_ids[None, :]).astype(jnp.float32)
    local_sum = jnp.dot(
        same_cluster,
        label_rows,
        precision=lax.Precision.HIGH,
        preferred_element_type=jnp.float32,
    )
    above = shard > here
    first_sum = jnp.sum(jnp.where((cluster_ids == first_id[here])[:, None], label_rows, 0.0), axis=0)
    last_sum = jnp.sum(jnp.where((cluster_ids == last_id[here])[:, None], label_rows, 0.0), axis=0)
    sending = jnp.where(above[:, None], last_sum[None, :], first_sum[None, :])
    lanes = 128
    gathered = lax.all_to_all(
        sending.reshape(width, -1, lanes), "label", 0, 0, tiled=True
    ).reshape(width, -1)

    doc_unit = unit_rows(features)
    row_scores = lax.dot_general(
        doc_unit,
        label_rows,
        (((1,), (1,)), ((), ())),
        precision=lax.Precision.HIGH,
        preferred_element_type=jnp.float32,
    )
    below = shard < here
    take_below = (last_id[None, :] == cluster_ids[:, None]) & below[None, :]
    take_above = (first_id[None, :] == cluster_ids[:, None]) & above[None, :]
    weights = take_below | take_above
    cluster_sum = local_sum + jnp.dot(
        weights.astype(jnp.float32),
        gathered,
        precision=lax.Precision.HIGH,
        preferred_element_type=jnp.float32,
    )
    centroid = unit_rows(cluster_sum)
    return lax.dot_general(
        doc_unit,
        centroid,
        (((1,), (1,)), ((), ())),
        precision=lax.Precision.HIGH,
        preferred_element_type=jnp.float32,
    ) + row_scores


def solution(mesh):
    doc = mesh.shape["doc"]
    split = Mesh(mesh.devices.reshape(doc // 2, 2, -1), ("dy", "dc", "label"))
    docs = ("dy", "dc")
    in_specs = (P(docs, None), P(docs, None), P(), P())
    out_specs = P(docs, "label")
    return jax.shard_map(shards, mesh=split, in_specs=in_specs, out_specs=out_specs, check_vma=False)
```

```python
import jax
import jax.numpy as jnp
from jax import lax
from jax.sharding import Mesh, PartitionSpec as P

L_DEV = 256


EPS = 1e-06


def unit_rows(matrix):
    return matrix * lax.rsqrt(jnp.sum(matrix * matrix, axis=1, keepdims=True) + EPS)


def cluster_of(positions, starts):
    return jnp.sum((starts[None, 1:] <= positions[:, None]).astype(jnp.int32), axis=1)


def shards(features, doc_labels, tree_perm, cluster_sizes):
    width = lax.axis_size("label")
    here = lax.axis_index("label")
    base = here * L_DEV
    slots = jnp.arange(L_DEV, dtype=jnp.int32)

    own_perm = lax.dynamic_slice_in_dim(tree_perm, base, L_DEV)
    incidence = jnp.sum(
        (doc_labels.T[:, None, :] == own_perm[None, :, None]).astype(jnp.float32), axis=0
    )
    partial_value = jnp.dot(
        incidence, features, precision=lax.Precision.HIGH, preferred_element_type=jnp.float32
    )
    chips = lax.axis_size("dy")
    depth = features.shape[1]
    half = L_DEV // 2
    core = lax.axis_index("dc")
    sibling = [(0, 1), (1, 0)]
    halves = partial_value.reshape(2, half, depth)
    keep = jnp.where(core == 0, halves[0], halves[1])
    give = jnp.where(core == 0, halves[1], halves[0])
    chip_half = keep + lax.ppermute(give, "dc", sibling)
    pieces = lax.all_to_all(
        chip_half.reshape(chips, half // chips, depth), "dy", 0, 0, tiled=True
    )
    mine = unit_rows(jnp.sum(pieces, axis=0))
    own_half = lax.all_to_all(
        jnp.broadcast_to(mine[None], (chips,) + mine.shape), "dy", 0, 0, tiled=True
    ).reshape(half, depth)
    other_half = lax.ppermute(own_half, "dc", sibling)
    label_rows = jnp.where(
        core == 0,
        jnp.concatenate([own_half, other_half]),
        jnp.concatenate([other_half, own_half]),
    )

    starts = jnp.cumsum(cluster_sizes) - cluster_sizes
    cluster_ids = cluster_of(base + slots, starts)
    shard = jnp.arange(width, dtype=jnp.int32)
    first_id = cluster_of(shard * L_DEV, starts)
    last_id = cluster_of(shard * L_DEV + (L_DEV - 1), starts)

    same_cluster = (cluster_ids[:, None] == cluster_ids[None, :]).astype(jnp.float32)
    local_sum = jnp.dot(
        same_cluster,
        label_rows,
        precision=lax.Precision.HIGH,
        preferred_element_type=jnp.float32,
    )
    above = shard > here
    first_sum = jnp.sum(jnp.where((cluster_ids == first_id[here])[:, None], label_rows, 0.0), axis=0)
    last_sum = jnp.sum(jnp.where((cluster_ids == last_id[here])[:, None], label_rows, 0.0), axis=0)
    sending = jnp.where(above[:, None], last_sum[None, :], first_sum[None, :])
    lanes = lax.axis_size("dy") * 2
    lane = lax.axis_index("dy") * 2 + core
    slice_width = depth // lanes
    mine_slice = lax.dynamic_slice_in_dim(sending, lane * slice_width, slice_width, axis=1)
    got = lax.all_to_all(mine_slice, "label", 0, 0, tiled=True)
    slices = lax.all_to_all(
        jnp.broadcast_to(got[None], (lanes,) + got.shape), ("dy", "dc"), 0, 0, tiled=True
    )
    gathered = jnp.transpose(slices, (1, 0, 2)).reshape(width, depth)

    doc_unit = unit_rows(features)
    row_scores = lax.dot_general(
        doc_unit,
        label_rows,
        (((1,), (1,)), ((), ())),
        precision=lax.Precision.HIGH,
        preferred_element_type=jnp.float32,
    )
    below = shard < here
    take_below = (last_id[None, :] == cluster_ids[:, None]) & below[None, :]
    take_above = (first_id[None, :] == cluster_ids[:, None]) & above[None, :]
    weights = take_below | take_above
    cluster_sum = local_sum + jnp.dot(
        weights.astype(jnp.float32),
        gathered,
        precision=lax.Precision.HIGH,
        preferred_element_type=jnp.float32,
    )
    centroid = unit_rows(cluster_sum)
    return lax.dot_general(
        doc_unit,
        centroid,
        (((1,), (1,)), ((), ())),
        precision=lax.Precision.HIGH,
        preferred_element_type=jnp.float32,
    ) + row_scores


def solution(mesh):
    doc = mesh.shape["doc"]
    split = Mesh(mesh.devices.reshape(doc // 2, 2, -1), ("dy", "dc", "label"))
    docs = ("dy", "dc")
    in_specs = (P(docs, None), P(docs, None), P(), P())
    out_specs = P(docs, "label")
    return jax.shard_map(shards, mesh=split, in_specs=in_specs, out_specs=out_specs, check_vma=False)
```

```python
import jax
import jax.numpy as jnp
from jax import lax
from jax.sharding import Mesh, PartitionSpec as P

L_DEV = 256


EPS = 1e-06


def unit_rows(matrix):
    return matrix * lax.rsqrt(jnp.sum(matrix * matrix, axis=1, keepdims=True) + EPS)


def cluster_of(positions, starts):
    return jnp.sum((starts[None, 1:] <= positions[:, None]).astype(jnp.int32), axis=1)


def shards(features, doc_labels, tree_perm, cluster_sizes):
    width = lax.axis_size("label")
    here = lax.axis_index("label")
    base = here * L_DEV
    slots = jnp.arange(L_DEV, dtype=jnp.int32)

    own_perm = lax.dynamic_slice_in_dim(tree_perm, base, L_DEV)
    incidence = jnp.sum(
        (doc_labels.T[:, None, :] == own_perm[None, :, None]).astype(jnp.float32), axis=0
    )
    partial_value = jnp.dot(
        incidence, features, precision=lax.Precision.HIGH, preferred_element_type=jnp.float32
    )
    chips = lax.axis_size("dy")
    depth = features.shape[1]
    half = L_DEV // 2
    core = lax.axis_index("dc")
    sibling = [(0, 1), (1, 0)]
    halves = partial_value.reshape(2, half, depth)
    keep = jnp.where(core == 0, halves[0], halves[1])
    give = jnp.where(core == 0, halves[1], halves[0])
    chip_half = keep + lax.ppermute(give, "dc", sibling)
    pieces = lax.all_to_all(
        chip_half.reshape(chips, half // chips, depth), "dy", 0, 0, tiled=True
    )
    mine = unit_rows(jnp.sum(pieces, axis=0))
    own_half = lax.all_to_all(
        jnp.broadcast_to(mine[None], (chips,) + mine.shape), "dy", 0, 0, tiled=True
    ).reshape(half, depth)
    other_half = lax.ppermute(own_half, "dc", sibling)
    label_rows = jnp.where(
        core == 0,
        jnp.concatenate([own_half, other_half]),
        jnp.concatenate([other_half, own_half]),
    )

    starts = jnp.cumsum(cluster_sizes) - cluster_sizes
    cluster_ids = cluster_of(base + slots, starts)
    shard = jnp.arange(width, dtype=jnp.int32)
    first_id = cluster_of(shard * L_DEV, starts)
    last_id = cluster_of(shard * L_DEV + (L_DEV - 1), starts)

    same_cluster = (cluster_ids[:, None] == cluster_ids[None, :]).astype(jnp.float32)
    local_sum = jnp.dot(
        same_cluster,
        label_rows,
        precision=lax.Precision.HIGH,
        preferred_element_type=jnp.float32,
    )
    above = shard > here
    first_sum = jnp.sum(jnp.where((cluster_ids == first_id[here])[:, None], label_rows, 0.0), axis=0)
    last_sum = jnp.sum(jnp.where((cluster_ids == last_id[here])[:, None], label_rows, 0.0), axis=0)
    sending = jnp.where(above[:, None], last_sum[None, :], first_sum[None, :])
    lanes = 128
    gathered = lax.all_to_all(
        sending.reshape(width, -1, lanes), "label", 0, 0, tiled=True
    ).reshape(width, -1)

    doc_unit = unit_rows(features)
    own_scores, other_scores = (
        lax.dot_general(
            doc_unit,
            rows,
            (((1,), (1,)), ((), ())),
            precision=lax.Precision.HIGH,
            preferred_element_type=jnp.float32,
        )
        for rows in (own_half, other_half)
    )
    row_scores = jnp.where(
        core == 0,
        jnp.concatenate([own_scores, other_scores], axis=1),
        jnp.concatenate([other_scores, own_scores], axis=1),
    )
    below = shard < here
    take_below = (last_id[None, :] == cluster_ids[:, None]) & below[None, :]
    take_above = (first_id[None, :] == cluster_ids[:, None]) & above[None, :]
    weights = take_below | take_above
    cluster_sum = local_sum + jnp.dot(
        weights.astype(jnp.float32),
        gathered,
        precision=lax.Precision.HIGH,
        preferred_element_type=jnp.float32,
    )
    centroid = unit_rows(cluster_sum)
    return lax.dot_general(
        doc_unit,
        centroid,
        (((1,), (1,)), ((), ())),
        precision=lax.Precision.HIGH,
        preferred_element_type=jnp.float32,
    ) + row_scores


def solution(mesh):
    doc = mesh.shape["doc"]
    split = Mesh(mesh.devices.reshape(doc // 2, 2, -1), ("dy", "dc", "label"))
    docs = ("dy", "dc")
    in_specs = (P(docs, None), P(docs, None), P(), P())
    out_specs = P(docs, "label")
    return jax.shard_map(shards, mesh=split, in_specs=in_specs, out_specs=out_specs, check_vma=False)
```

```python
import jax
import jax.numpy as jnp
from jax import lax
from jax.sharding import Mesh, PartitionSpec as P

L_DEV = 256


EPS = 1e-06


def unit_rows(matrix):
    return matrix * lax.rsqrt(jnp.sum(matrix * matrix, axis=1, keepdims=True) + EPS)


def cluster_of(positions, starts):
    return jnp.sum((starts[None, 1:] <= positions[:, None]).astype(jnp.int32), axis=1)


def shards(features, doc_labels, tree_perm, cluster_sizes):
    width = lax.axis_size("label")
    here = lax.axis_index("label")
    base = here * L_DEV
    slots = jnp.arange(L_DEV, dtype=jnp.int32)

    own_perm = lax.dynamic_slice_in_dim(tree_perm, base, L_DEV)
    incidence = jnp.sum(
        (doc_labels.T[:, None, :] == own_perm[None, :, None]).astype(jnp.float32), axis=0
    )
    partial_value = jnp.dot(
        incidence, features, precision=lax.Precision.HIGH, preferred_element_type=jnp.float32
    )
    chips = lax.axis_size("dy")
    depth = features.shape[1]
    half = L_DEV // 2
    core = lax.axis_index("dc")
    sibling = [(0, 1), (1, 0)]
    halves = partial_value.reshape(2, half, depth)
    keep = jnp.where(core == 0, halves[0], halves[1])
    give = jnp.where(core == 0, halves[1], halves[0])
    chip_half = keep + lax.ppermute(give, "dc", sibling)
    pieces = lax.all_to_all(
        chip_half.reshape(chips, half // chips, depth), "dy", 0, 0, tiled=True
    )
    mine = unit_rows(jnp.sum(pieces, axis=0))
    own_half = lax.all_to_all(
        jnp.broadcast_to(mine[None], (chips,) + mine.shape), "dy", 0, 0, tiled=True
    ).reshape(half, depth)
    other_half = lax.ppermute(own_half, "dc", sibling)
    label_rows = jnp.where(
        core == 0,
        jnp.concatenate([own_half, other_half]),
        jnp.concatenate([other_half, own_half]),
    )

    starts = jnp.cumsum(cluster_sizes) - cluster_sizes
    cluster_ids = cluster_of(base + slots, starts)
    shard = jnp.arange(width, dtype=jnp.int32)
    first_id = cluster_of(shard * L_DEV, starts)
    last_id = cluster_of(shard * L_DEV + (L_DEV - 1), starts)

    half_ids = (
        cluster_of(base + core * half + jnp.arange(half), starts),
        cluster_of(base + (1 - core) * half + jnp.arange(half), starts),
    )
    local_sum = sum(
        jnp.dot(
            (cluster_ids[:, None] == ids[None, :]).astype(jnp.float32),
            rows,
            precision=lax.Precision.HIGH,
            preferred_element_type=jnp.float32,
        )
        for ids, rows in zip(half_ids, (own_half, other_half))
    )
    above = shard > here
    first_sum = jnp.sum(jnp.where((cluster_ids == first_id[here])[:, None], label_rows, 0.0), axis=0)
    last_sum = jnp.sum(jnp.where((cluster_ids == last_id[here])[:, None], label_rows, 0.0), axis=0)
    sending = jnp.where(above[:, None], last_sum[None, :], first_sum[None, :])
    lanes = 128
    gathered = lax.all_to_all(
        sending.reshape(width, -1, lanes), "label", 0, 0, tiled=True
    ).reshape(width, -1)

    doc_unit = unit_rows(features)
    own_scores, other_scores = (
        lax.dot_general(
            doc_unit,
            rows,
            (((1,), (1,)), ((), ())),
            precision=lax.Precision.HIGH,
            preferred_element_type=jnp.float32,
        )
        for rows in (own_half, other_half)
    )
    row_scores = jnp.where(
        core == 0,
        jnp.concatenate([own_scores, other_scores], axis=1),
        jnp.concatenate([other_scores, own_scores], axis=1),
    )
    below = shard < here
    take_below = (last_id[None, :] == cluster_ids[:, None]) & below[None, :]
    take_above = (first_id[None, :] == cluster_ids[:, None]) & above[None, :]
    weights = take_below | take_above
    cluster_sum = local_sum + jnp.dot(
        weights.astype(jnp.float32),
        gathered,
        precision=lax.Precision.HIGH,
        preferred_element_type=jnp.float32,
    )
    centroid = unit_rows(cluster_sum)
    return lax.dot_general(
        doc_unit,
        centroid,
        (((1,), (1,)), ((), ())),
        precision=lax.Precision.HIGH,
        preferred_element_type=jnp.float32,
    ) + row_scores


def solution(mesh):
    doc = mesh.shape["doc"]
    split = Mesh(mesh.devices.reshape(doc // 2, 2, -1), ("dy", "dc", "label"))
    docs = ("dy", "dc")
    in_specs = (P(docs, None), P(docs, None), P(), P())
    out_specs = P(docs, "label")
    return jax.shard_map(shards, mesh=split, in_specs=in_specs, out_specs=out_specs, check_vma=False)
```

```python
import jax
import jax.numpy as jnp
from jax import lax
from jax.sharding import Mesh, PartitionSpec as P

L_DEV = 256


EPS = 1e-06


def unit_rows(matrix):
    return matrix * lax.rsqrt(jnp.sum(matrix * matrix, axis=1, keepdims=True) + EPS)


def cluster_of(positions, starts):
    return jnp.sum((starts[None, 1:] <= positions[:, None]).astype(jnp.int32), axis=1)


def shards(features, doc_labels, tree_perm, cluster_sizes):
    width = lax.axis_size("label")
    here = lax.axis_index("label")
    base = here * L_DEV
    slots = jnp.arange(L_DEV, dtype=jnp.int32)

    chips = lax.axis_size("dy")
    depth = features.shape[1]
    half = L_DEV // 2
    core = lax.axis_index("dc")
    sibling = [(0, 1), (1, 0)]

    def partial_rows(start):
        labels = lax.dynamic_slice_in_dim(tree_perm, start, half)
        incidence = jnp.sum(
            (doc_labels.T[:, None, :] == labels[None, :, None]).astype(jnp.float32), axis=0
        )
        return jnp.dot(
            incidence, features, precision=lax.Precision.HIGH, preferred_element_type=jnp.float32
        )

    given = lax.ppermute(partial_rows(base + (1 - core) * half), "dc", sibling)
    (kept,) = lax.optimization_barrier((partial_rows(base + core * half),))
    chip_half = kept + given
    pieces = lax.all_to_all(
        chip_half.reshape(chips, half // chips, depth), "dy", 0, 0, tiled=True
    )
    mine = unit_rows(jnp.sum(pieces, axis=0))
    own_half = lax.all_to_all(
        jnp.broadcast_to(mine[None], (chips,) + mine.shape), "dy", 0, 0, tiled=True
    ).reshape(half, depth)
    other_half = lax.ppermute(own_half, "dc", sibling)
    label_rows = jnp.where(
        core == 0,
        jnp.concatenate([own_half, other_half]),
        jnp.concatenate([other_half, own_half]),
    )

    starts = jnp.cumsum(cluster_sizes) - cluster_sizes
    cluster_ids = cluster_of(base + slots, starts)
    shard = jnp.arange(width, dtype=jnp.int32)
    first_id = cluster_of(shard * L_DEV, starts)
    last_id = cluster_of(shard * L_DEV + (L_DEV - 1), starts)

    half_ids = (
        cluster_of(base + core * half + jnp.arange(half), starts),
        cluster_of(base + (1 - core) * half + jnp.arange(half), starts),
    )
    local_sum = sum(
        jnp.dot(
            (cluster_ids[:, None] == ids[None, :]).astype(jnp.float32),
            rows,
            precision=lax.Precision.HIGH,
            preferred_element_type=jnp.float32,
        )
        for ids, rows in zip(half_ids, (own_half, other_half))
    )
    above = shard > here
    first_sum = jnp.sum(jnp.where((cluster_ids == first_id[here])[:, None], label_rows, 0.0), axis=0)
    last_sum = jnp.sum(jnp.where((cluster_ids == last_id[here])[:, None], label_rows, 0.0), axis=0)
    sending = jnp.where(above[:, None], last_sum[None, :], first_sum[None, :])
    lanes = 128
    gathered = lax.all_to_all(
        sending.reshape(width, -1, lanes), "label", 0, 0, tiled=True
    ).reshape(width, -1)

    doc_unit = unit_rows(features)
    own_scores, other_scores = (
        lax.dot_general(
            doc_unit,
            rows,
            (((1,), (1,)), ((), ())),
            precision=lax.Precision.HIGH,
            preferred_element_type=jnp.float32,
        )
        for rows in (own_half, other_half)
    )
    row_scores = jnp.where(
        core == 0,
        jnp.concatenate([own_scores, other_scores], axis=1),
        jnp.concatenate([other_scores, own_scores], axis=1),
    )
    below = shard < here
    take_below = (last_id[None, :] == cluster_ids[:, None]) & below[None, :]
    take_above = (first_id[None, :] == cluster_ids[:, None]) & above[None, :]
    weights = take_below | take_above
    cluster_sum = local_sum + jnp.dot(
        weights.astype(jnp.float32),
        gathered,
        precision=lax.Precision.HIGH,
        preferred_element_type=jnp.float32,
    )
    centroid = unit_rows(cluster_sum)
    return lax.dot_general(
        doc_unit,
        centroid,
        (((1,), (1,)), ((), ())),
        precision=lax.Precision.HIGH,
        preferred_element_type=jnp.float32,
    ) + row_scores


def solution(mesh):
    doc = mesh.shape["doc"]
    split = Mesh(mesh.devices.reshape(doc // 2, 2, -1), ("dy", "dc", "label"))
    docs = ("dy", "dc")
    in_specs = (P(docs, None), P(docs, None), P(), P())
    out_specs = P(docs, "label")
    return jax.shard_map(shards, mesh=split, in_specs=in_specs, out_specs=out_specs, check_vma=False)
```

```python
import jax
import jax.numpy as jnp
from jax import lax
from jax.sharding import Mesh, PartitionSpec as P

L_DEV = 256


EPS = 1e-06


def unit_rows(matrix):
    return matrix * lax.rsqrt(jnp.sum(matrix * matrix, axis=1, keepdims=True) + EPS)


def cluster_of(positions, starts):
    return jnp.sum((starts[None, 1:] <= positions[:, None]).astype(jnp.int32), axis=1)


def shards(features, doc_labels, tree_perm, cluster_sizes):
    width = lax.axis_size("label")
    here = lax.axis_index("label")
    base = here * L_DEV
    slots = jnp.arange(L_DEV, dtype=jnp.int32)

    own_perm = lax.dynamic_slice_in_dim(tree_perm, base, L_DEV)
    incidence = jnp.sum(
        (doc_labels.T[:, None, :] == own_perm[None, :, None]).astype(jnp.float32), axis=0
    )
    partial_value = jnp.dot(
        incidence, features, precision=lax.Precision.HIGH, preferred_element_type=jnp.float32
    )
    chips = lax.axis_size("dy")
    depth = features.shape[1]
    half = L_DEV // 2
    core = lax.axis_index("dc")
    sibling = [(0, 1), (1, 0)]
    halves = partial_value.reshape(2, half, depth)
    keep = jnp.where(core == 0, halves[0], halves[1])
    give = jnp.where(core == 0, halves[1], halves[0])
    chip_half = keep + lax.ppermute(give, "dc", sibling)
    pieces = lax.all_to_all(
        chip_half.reshape(chips, half // chips, depth), "dy", 0, 0, tiled=True
    )
    mine = unit_rows(jnp.sum(pieces, axis=0))
    own_half = lax.all_to_all(
        jnp.broadcast_to(mine[None], (chips,) + mine.shape), "dy", 0, 0, tiled=True
    ).reshape(half, depth)
    other_half = lax.ppermute(own_half, "dc", sibling)
    label_rows = jnp.where(
        core == 0,
        jnp.concatenate([own_half, other_half]),
        jnp.concatenate([other_half, own_half]),
    )

    starts = jnp.cumsum(cluster_sizes) - cluster_sizes
    cluster_ids = cluster_of(base + slots, starts)
    shard = jnp.arange(width, dtype=jnp.int32)
    first_id = cluster_of(shard * L_DEV, starts)
    last_id = cluster_of(shard * L_DEV + (L_DEV - 1), starts)

    half_ids = (
        cluster_of(base + core * half + jnp.arange(half), starts),
        cluster_of(base + (1 - core) * half + jnp.arange(half), starts),
    )
    local_sum = sum(
        jnp.dot(
            (cluster_ids[:, None] == ids[None, :]).astype(jnp.float32),
            rows,
            precision=lax.Precision.HIGH,
            preferred_element_type=jnp.float32,
        )
        for ids, rows in zip(half_ids, (own_half, other_half))
    )
    above = shard > here
    first_sum = jnp.sum(jnp.where((cluster_ids == first_id[here])[:, None], label_rows, 0.0), axis=0)
    last_sum = jnp.sum(jnp.where((cluster_ids == last_id[here])[:, None], label_rows, 0.0), axis=0)
    sending = jnp.where(above[:, None], last_sum[None, :], first_sum[None, :])
    lanes = 128
    gathered = lax.all_to_all(
        sending.reshape(width, -1, lanes), "label", 0, 0, tiled=True
    ).reshape(width, -1)

    doc_unit = unit_rows(features)
    own_scores, other_scores = (
        lax.dot_general(
            doc_unit,
            rows,
            (((1,), (1,)), ((), ())),
            precision=lax.Precision.HIGH,
            preferred_element_type=jnp.float32,
        )
        for rows in (own_half, other_half)
    )
    row_scores = jnp.where(
        core == 0,
        jnp.concatenate([own_scores, other_scores], axis=1),
        jnp.concatenate([other_scores, own_scores], axis=1),
    )
    below = shard < here
    extras = []
    for target in (first_id[here], last_id[here]):
        use = (below & (last_id == target)) | (above & (first_id == target))
        extras.append(jnp.sum(jnp.where(use[:, None], gathered, 0.0), axis=0))
    in_first = (cluster_ids == first_id[here])[:, None]
    in_last = (cluster_ids == last_id[here])[:, None]
    cluster_sum = local_sum + jnp.where(
        in_first, extras[0][None, :], jnp.where(in_last, extras[1][None, :], 0.0)
    )
    centroid = unit_rows(cluster_sum)
    return lax.dot_general(
        doc_unit,
        centroid,
        (((1,), (1,)), ((), ())),
        precision=lax.Precision.HIGH,
        preferred_element_type=jnp.float32,
    ) + row_scores


def solution(mesh):
    doc = mesh.shape["doc"]
    split = Mesh(mesh.devices.reshape(doc // 2, 2, -1), ("dy", "dc", "label"))
    docs = ("dy", "dc")
    in_specs = (P(docs, None), P(docs, None), P(), P())
    out_specs = P(docs, "label")
    return jax.shard_map(shards, mesh=split, in_specs=in_specs, out_specs=out_specs, check_vma=False)
```

```python
import jax
import jax.numpy as jnp
from jax import lax
from jax.sharding import Mesh, PartitionSpec as P

L_DEV = 256


EPS = 1e-06


def unit_rows(matrix):
    return matrix * lax.rsqrt(jnp.sum(matrix * matrix, axis=1, keepdims=True) + EPS)


def cluster_of(positions, starts):
    return jnp.sum((starts[None, 1:] <= positions[:, None]).astype(jnp.int32), axis=1)


def shards(features, doc_labels, tree_perm, cluster_sizes):
    width = lax.axis_size("label")
    here = lax.axis_index("label")
    base = here * L_DEV
    slots = jnp.arange(L_DEV, dtype=jnp.int32)

    own_perm = lax.dynamic_slice_in_dim(tree_perm, base, L_DEV)
    incidence = jnp.sum(
        (doc_labels.T[:, None, :] == own_perm[None, :, None]).astype(jnp.float32), axis=0
    )
    partial_value = jnp.dot(
        incidence, features, precision=lax.Precision.HIGH, preferred_element_type=jnp.float32
    )
    chips = lax.axis_size("dy")
    depth = features.shape[1]
    half = L_DEV // 2
    core = lax.axis_index("dc")
    sibling = [(0, 1), (1, 0)]
    halves = partial_value.reshape(2, half, depth)
    keep = jnp.where(core == 0, halves[0], halves[1])
    give = jnp.where(core == 0, halves[1], halves[0])
    chip_half = keep + lax.ppermute(give, "dc", sibling)
    pieces = lax.all_to_all(
        chip_half.reshape(chips, half // chips, depth), "dy", 0, 0, tiled=True
    )
    mine = unit_rows(jnp.sum(pieces, axis=0))
    own_half = lax.all_to_all(
        jnp.broadcast_to(mine[None], (chips,) + mine.shape), "dy", 0, 0, tiled=True
    ).reshape(half, depth)
    other_half = lax.ppermute(own_half, "dc", sibling)
    label_rows = jnp.where(
        core == 0,
        jnp.concatenate([own_half, other_half]),
        jnp.concatenate([other_half, own_half]),
    )

    starts = jnp.cumsum(cluster_sizes) - cluster_sizes
    cluster_ids = cluster_of(base + slots, starts)
    shard = jnp.arange(width, dtype=jnp.int32)
    first_id = cluster_of(shard * L_DEV, starts)
    last_id = cluster_of(shard * L_DEV + (L_DEV - 1), starts)

    half_ids = (
        cluster_of(base + core * half + jnp.arange(half), starts),
        cluster_of(base + (1 - core) * half + jnp.arange(half), starts),
    )
    local_sum = sum(
        jnp.dot(
            (cluster_ids[:, None] == ids[None, :]).astype(jnp.float32),
            rows,
            precision=lax.Precision.HIGH,
            preferred_element_type=jnp.float32,
        )
        for ids, rows in zip(half_ids, (own_half, other_half))
    )
    above = shard > here
    first_sum = jnp.sum(jnp.where((cluster_ids == first_id[here])[:, None], label_rows, 0.0), axis=0)
    last_sum = jnp.sum(jnp.where((cluster_ids == last_id[here])[:, None], label_rows, 0.0), axis=0)
    sending = jnp.where(above[:, None], last_sum[None, :], first_sum[None, :])
    lanes = 128
    gathered = lax.all_to_all(
        sending.reshape(width, -1, lanes), "label", 0, 0, tiled=True
    ).reshape(width, -1)

    doc_unit = unit_rows(features)
    own_scores, other_scores = (
        lax.dot_general(
            doc_unit,
            rows,
            (((1,), (1,)), ((), ())),
            precision=lax.Precision.HIGH,
            preferred_element_type=jnp.float32,
        )
        for rows in (own_half, other_half)
    )
    row_scores = jnp.where(
        core == 0,
        jnp.concatenate([own_scores, other_scores], axis=1),
        jnp.concatenate([other_scores, own_scores], axis=1),
    )
    local_scores = lax.dot_general(
        doc_unit,
        unit_rows(local_sum),
        (((1,), (1,)), ((), ())),
        precision=lax.Precision.HIGH,
        preferred_element_type=jnp.float32,
    )
    (local_scores,) = lax.optimization_barrier((local_scores,))
    below = shard < here
    targets = (first_id[here], last_id[here])
    use = jnp.stack(
        [(below & (last_id == t)) | (above & (first_id == t)) for t in targets]
    ).astype(jnp.float32)
    end_sums = jnp.stack([local_sum[0], local_sum[-1]]) + jnp.dot(
        use, gathered, precision=lax.Precision.HIGH, preferred_element_type=jnp.float32
    )
    end_scores = lax.dot_general(
        doc_unit,
        unit_rows(end_sums),
        (((1,), (1,)), ((), ())),
        precision=lax.Precision.HIGH,
        preferred_element_type=jnp.float32,
    )
    in_first = (cluster_ids == targets[0])[None, :]
    in_last = (cluster_ids == targets[1])[None, :]
    centroid_scores = jnp.where(
        in_first, end_scores[:, :1], jnp.where(in_last, end_scores[:, 1:], local_scores)
    )
    return centroid_scores + row_scores

def solution(mesh):
    doc = mesh.shape["doc"]
    split = Mesh(mesh.devices.reshape(doc // 2, 2, -1), ("dy", "dc", "label"))
    docs = ("dy", "dc")
    in_specs = (P(docs, None), P(docs, None), P(), P())
    out_specs = P(docs, "label")
    return jax.shard_map(shards, mesh=split, in_specs=in_specs, out_specs=out_specs, check_vma=False)
```

```python
import jax
import jax.numpy as jnp
from jax import lax
from jax.sharding import Mesh, PartitionSpec as P

L_DEV = 256


EPS = 1e-06


def unit_rows(matrix):
    return matrix * lax.rsqrt(jnp.sum(matrix * matrix, axis=1, keepdims=True) + EPS)


def cluster_of(positions, starts):
    return jnp.sum((starts[None, 1:] <= positions[:, None]).astype(jnp.int32), axis=1)


def shards(features, doc_labels, tree_perm, cluster_sizes):
    width = lax.axis_size("label")
    here = lax.axis_index("label")
    base = here * L_DEV
    slots = jnp.arange(L_DEV, dtype=jnp.int32)

    own_perm = lax.dynamic_slice_in_dim(tree_perm, base, L_DEV)
    incidence = jnp.sum(
        (doc_labels.T[:, None, :] == own_perm[None, :, None]).astype(jnp.float32), axis=0
    )
    partial_value = jnp.dot(
        incidence, features, precision=lax.Precision.HIGH, preferred_element_type=jnp.float32
    )
    chips = lax.axis_size("dy")
    depth = features.shape[1]
    half = L_DEV // 2
    core = lax.axis_index("dc")
    sibling = [(0, 1), (1, 0)]
    keep = lax.dynamic_slice_in_dim(partial_value, core * half, half)
    give = lax.dynamic_slice_in_dim(partial_value, (1 - core) * half, half)
    chip_half = keep + lax.ppermute(give, "dc", sibling)
    pieces = lax.all_to_all(
        chip_half.reshape(chips, half // chips, depth), "dy", 0, 0, tiled=True
    )
    mine = unit_rows(jnp.sum(pieces, axis=0))
    own_half = lax.all_to_all(
        jnp.broadcast_to(mine[None], (chips,) + mine.shape), "dy", 0, 0, tiled=True
    ).reshape(half, depth)
    other_half = lax.ppermute(own_half, "dc", sibling)

    starts = jnp.cumsum(cluster_sizes) - cluster_sizes
    cluster_ids = cluster_of(base + slots, starts)
    shard = jnp.arange(width, dtype=jnp.int32)
    first_id = cluster_of(shard * L_DEV, starts)
    last_id = cluster_of(shard * L_DEV + (L_DEV - 1), starts)

    half_ids = (
        cluster_of(base + core * half + jnp.arange(half), starts),
        cluster_of(base + (1 - core) * half + jnp.arange(half), starts),
    )
    local_sum = sum(
        jnp.dot(
            (cluster_ids[:, None] == ids[None, :]).astype(jnp.float32),
            rows,
            precision=lax.Precision.HIGH,
            preferred_element_type=jnp.float32,
        )
        for ids, rows in zip(half_ids, (own_half, other_half))
    )
    above = shard > here
    first_sum, last_sum = (
        sum(
            jnp.sum(jnp.where((ids == target)[:, None], rows, 0.0), axis=0)
            for ids, rows in zip(half_ids, (own_half, other_half))
        )
        for target in (first_id[here], last_id[here])
    )
    sending = jnp.where(above[:, None], last_sum[None, :], first_sum[None, :])
    lanes = 128
    gathered = lax.all_to_all(
        sending.reshape(width, -1, lanes), "label", 0, 0, tiled=True
    ).reshape(width, -1)

    doc_unit = unit_rows(features)
    own_scores, other_scores = (
        lax.dot_general(
            doc_unit,
            rows,
            (((1,), (1,)), ((), ())),
            precision=lax.Precision.HIGH,
            preferred_element_type=jnp.float32,
        )
        for rows in (own_half, other_half)
    )
    row_scores = jnp.where(
        core == 0,
        jnp.concatenate([own_scores, other_scores], axis=1),
        jnp.concatenate([other_scores, own_scores], axis=1),
    )
    below = shard < here
    take_below = (last_id[None, :] == cluster_ids[:, None]) & below[None, :]
    take_above = (first_id[None, :] == cluster_ids[:, None]) & above[None, :]
    weights = take_below | take_above
    cluster_sum = local_sum + jnp.dot(
        weights.astype(jnp.float32),
        gathered,
        precision=lax.Precision.HIGH,
        preferred_element_type=jnp.float32,
    )
    centroid = unit_rows(cluster_sum)
    return lax.dot_general(
        doc_unit,
        centroid,
        (((1,), (1,)), ((), ())),
        precision=lax.Precision.HIGH,
        preferred_element_type=jnp.float32,
    ) + row_scores


def solution(mesh):
    doc = mesh.shape["doc"]
    split = Mesh(mesh.devices.reshape(doc // 2, 2, -1), ("dy", "dc", "label"))
    docs = ("dy", "dc")
    in_specs = (P(docs, None), P(docs, None), P(), P())
    out_specs = P(docs, "label")
    return jax.shard_map(shards, mesh=split, in_specs=in_specs, out_specs=out_specs, check_vma=False)
```

```python
import jax
import jax.numpy as jnp
from jax import lax
from jax.sharding import Mesh, PartitionSpec as P

L_DEV = 256


EPS = 1e-06


def exact_left_dot(a, b):
    a = a.astype(jnp.bfloat16)
    scaled = b * 65537.0
    high = scaled - (scaled - b)
    low = b - high
    return jnp.dot(a, high.astype(jnp.bfloat16), preferred_element_type=jnp.float32) + jnp.dot(
        a, low.astype(jnp.bfloat16), preferred_element_type=jnp.float32
    )


def unit_rows(matrix):
    return matrix * lax.rsqrt(jnp.sum(matrix * matrix, axis=1, keepdims=True) + EPS)


def cluster_of(positions, starts):
    return jnp.sum((starts[None, 1:] <= positions[:, None]).astype(jnp.int32), axis=1)


def shards(features, doc_labels, tree_perm, cluster_sizes):
    width = lax.axis_size("label")
    here = lax.axis_index("label")
    base = here * L_DEV
    slots = jnp.arange(L_DEV, dtype=jnp.int32)

    own_perm = lax.dynamic_slice_in_dim(tree_perm, base, L_DEV)
    incidence = jnp.sum(
        (doc_labels.T[:, None, :] == own_perm[None, :, None]).astype(jnp.float32), axis=0
    )
    partial_value = exact_left_dot(incidence, features)
    chips = lax.axis_size("dy")
    depth = features.shape[1]
    half = L_DEV // 2
    core = lax.axis_index("dc")
    sibling = [(0, 1), (1, 0)]
    halves = partial_value.reshape(2, half, depth)
    keep = jnp.where(core == 0, halves[0], halves[1])
    give = jnp.where(core == 0, halves[1], halves[0])
    chip_half = keep + lax.ppermute(give, "dc", sibling)
    pieces = lax.all_to_all(
        chip_half.reshape(chips, half // chips, depth), "dy", 0, 0, tiled=True
    )
    mine = unit_rows(jnp.sum(pieces, axis=0))
    own_half = lax.all_to_all(
        jnp.broadcast_to(mine[None], (chips,) + mine.shape), "dy", 0, 0, tiled=True
    ).reshape(half, depth)
    other_half = lax.ppermute(own_half, "dc", sibling)
    label_rows = jnp.where(
        core == 0,
        jnp.concatenate([own_half, other_half]),
        jnp.concatenate([other_half, own_half]),
    )

    starts = jnp.cumsum(cluster_sizes) - cluster_sizes
    cluster_ids = cluster_of(base + slots, starts)
    shard = jnp.arange(width, dtype=jnp.int32)
    first_id = cluster_of(shard * L_DEV, starts)
    last_id = cluster_of(shard * L_DEV + (L_DEV - 1), starts)

    half_ids = (
        cluster_of(base + core * half + jnp.arange(half), starts),
        cluster_of(base + (1 - core) * half + jnp.arange(half), starts),
    )
    local_sum = sum(
        jnp.dot(
            (cluster_ids[:, None] == ids[None, :]).astype(jnp.float32),
            rows,
            precision=lax.Precision.HIGH,
            preferred_element_type=jnp.float32,
        )
        for ids, rows in zip(half_ids, (own_half, other_half))
    )
    above = shard > here
    first_sum = jnp.sum(jnp.where((cluster_ids == first_id[here])[:, None], label_rows, 0.0), axis=0)
    last_sum = jnp.sum(jnp.where((cluster_ids == last_id[here])[:, None], label_rows, 0.0), axis=0)
    sending = jnp.where(above[:, None], last_sum[None, :], first_sum[None, :])
    lanes = 128
    gathered = lax.all_to_all(
        sending.reshape(width, -1, lanes), "label", 0, 0, tiled=True
    ).reshape(width, -1)

    doc_unit = unit_rows(features)
    own_scores, other_scores = (
        lax.dot_general(
            doc_unit,
            rows,
            (((1,), (1,)), ((), ())),
            precision=lax.Precision.HIGH,
            preferred_element_type=jnp.float32,
        )
        for rows in (own_half, other_half)
    )
    row_scores = jnp.where(
        core == 0,
        jnp.concatenate([own_scores, other_scores], axis=1),
        jnp.concatenate([other_scores, own_scores], axis=1),
    )
    below = shard < here
    take_below = (last_id[None, :] == cluster_ids[:, None]) & below[None, :]
    take_above = (first_id[None, :] == cluster_ids[:, None]) & above[None, :]
    weights = take_below | take_above
    cluster_sum = local_sum + exact_left_dot(weights, gathered)
    centroid = unit_rows(cluster_sum)
    return lax.dot_general(
        doc_unit,
        centroid,
        (((1,), (1,)), ((), ())),
        precision=lax.Precision.HIGH,
        preferred_element_type=jnp.float32,
    ) + row_scores


def solution(mesh):
    doc = mesh.shape["doc"]
    split = Mesh(mesh.devices.reshape(doc // 2, 2, -1), ("dy", "dc", "label"))
    docs = ("dy", "dc")
    in_specs = (P(docs, None), P(docs, None), P(), P())
    out_specs = P(docs, "label")
    return jax.shard_map(shards, mesh=split, in_specs=in_specs, out_specs=out_specs, check_vma=False)
```

```python
import jax
import jax.numpy as jnp
from jax import lax
from jax.sharding import Mesh, PartitionSpec as P

L_DEV = 256


EPS = 1e-06


def unit_rows(matrix):
    return matrix * lax.rsqrt(jnp.sum(matrix * matrix, axis=1, keepdims=True) + EPS)


def cluster_of(positions, starts):
    return jnp.sum((starts[None, 1:] <= positions[:, None]).astype(jnp.int32), axis=1)


def shards(features, doc_labels, tree_perm, cluster_sizes):
    width = lax.axis_size("label")
    here = lax.axis_index("label")
    base = here * L_DEV
    slots = jnp.arange(L_DEV, dtype=jnp.int32)

    own_perm = lax.dynamic_slice_in_dim(tree_perm, base, L_DEV)
    incidence = jnp.sum(
        (doc_labels.T[:, None, :] == own_perm[None, :, None]).astype(jnp.float32), axis=0
    )
    partial_value = jnp.dot(
        incidence, features, precision=lax.Precision.HIGH, preferred_element_type=jnp.float32
    )
    chips = lax.axis_size("dy")
    depth = features.shape[1]
    half = L_DEV // 2
    core = lax.axis_index("dc")
    sibling = [(0, 1), (1, 0)]
    halves = partial_value.reshape(2, half, depth)
    keep = jnp.where(core == 0, halves[0], halves[1])
    give = jnp.where(core == 0, halves[1], halves[0])
    chip_half = keep + lax.ppermute(give, "dc", sibling)
    pieces = lax.all_to_all(
        chip_half.reshape(chips, half // chips, depth), "dy", 0, 0, tiled=True
    )
    mine = unit_rows(jnp.sum(pieces, axis=0))
    own_half = lax.all_to_all(
        jnp.broadcast_to(mine[None], (chips,) + mine.shape), "dy", 0, 0, tiled=True
    ).reshape(half, depth)
    other_half = lax.ppermute(own_half, "dc", sibling)
    label_rows = jnp.where(
        core == 0,
        jnp.concatenate([own_half, other_half]),
        jnp.concatenate([other_half, own_half]),
    )

    starts = jnp.cumsum(cluster_sizes) - cluster_sizes
    cluster_ids = cluster_of(base + slots, starts)
    shard = jnp.arange(width, dtype=jnp.int32)
    first_id = cluster_of(shard * L_DEV, starts)
    last_id = cluster_of(shard * L_DEV + (L_DEV - 1), starts)

    half_ids = (
        cluster_of(base + core * half + jnp.arange(half), starts),
        cluster_of(base + (1 - core) * half + jnp.arange(half), starts),
    )
    local_sum = sum(
        jnp.dot(
            (cluster_ids[:, None] == ids[None, :]).astype(jnp.float32),
            rows,
            precision=lax.Precision.HIGH,
            preferred_element_type=jnp.float32,
        )
        for ids, rows in zip(half_ids, (own_half, other_half))
    )
    above = shard > here
    first_sum = jnp.sum(jnp.where((cluster_ids == first_id[here])[:, None], label_rows, 0.0), axis=0)
    last_sum = jnp.sum(jnp.where((cluster_ids == last_id[here])[:, None], label_rows, 0.0), axis=0)
    sending = jnp.where(above[:, None], last_sum[None, :], first_sum[None, :])
    lanes = 128
    part = depth // 2
    got = lax.all_to_all(
        lax.dynamic_slice_in_dim(sending, core * part, part, axis=1).reshape(width, -1, lanes),
        "label",
        0,
        0,
        tiled=True,
    ).reshape(width, part)
    swapped = lax.ppermute(got, "dc", sibling)
    gathered = jnp.where(
        core == 0,
        jnp.concatenate([got, swapped], axis=1),
        jnp.concatenate([swapped, got], axis=1),
    )

    doc_unit = unit_rows(features)
    own_scores, other_scores = (
        lax.dot_general(
            doc_unit,
            rows,
            (((1,), (1,)), ((), ())),
            precision=lax.Precision.HIGH,
            preferred_element_type=jnp.float32,
        )
        for rows in (own_half, other_half)
    )
    row_scores = jnp.where(
        core == 0,
        jnp.concatenate([own_scores, other_scores], axis=1),
        jnp.concatenate([other_scores, own_scores], axis=1),
    )
    below = shard < here
    take_below = (last_id[None, :] == cluster_ids[:, None]) & below[None, :]
    take_above = (first_id[None, :] == cluster_ids[:, None]) & above[None, :]
    weights = take_below | take_above
    cluster_sum = local_sum + jnp.dot(
        weights.astype(jnp.float32),
        gathered,
        precision=lax.Precision.HIGH,
        preferred_element_type=jnp.float32,
    )
    centroid = unit_rows(cluster_sum)
    return lax.dot_general(
        doc_unit,
        centroid,
        (((1,), (1,)), ((), ())),
        precision=lax.Precision.HIGH,
        preferred_element_type=jnp.float32,
    ) + row_scores


def solution(mesh):
    doc = mesh.shape["doc"]
    split = Mesh(mesh.devices.reshape(doc // 2, 2, -1), ("dy", "dc", "label"))
    docs = ("dy", "dc")
    in_specs = (P(docs, None), P(docs, None), P(), P())
    out_specs = P(docs, "label")
    return jax.shard_map(shards, mesh=split, in_specs=in_specs, out_specs=out_specs, check_vma=False)
```

```python
import jax
import jax.numpy as jnp
from jax import lax
from jax.sharding import Mesh, PartitionSpec as P

L_DEV = 256


EPS = 1e-06


def unit_rows(matrix):
    return matrix * lax.rsqrt(jnp.sum(matrix * matrix, axis=1, keepdims=True) + EPS)


def cluster_of(positions, starts):
    return jnp.sum((starts[None, 1:] <= positions[:, None]).astype(jnp.int32), axis=1)


def shards(features, doc_labels, tree_perm, cluster_sizes):
    width = lax.axis_size("label")
    here = lax.axis_index("label")
    base = here * L_DEV
    slots = jnp.arange(L_DEV, dtype=jnp.int32)

    own_perm = lax.dynamic_slice_in_dim(tree_perm, base, L_DEV)
    incidence = jnp.sum(
        (doc_labels.T[:, None, :] == own_perm[None, :, None]).astype(jnp.float32), axis=0
    )
    partial_value = jnp.dot(
        incidence, features, precision=lax.Precision.HIGH, preferred_element_type=jnp.float32
    )
    chips = lax.axis_size("dy")
    depth = features.shape[1]
    half = L_DEV // 2
    core = lax.axis_index("dc")
    sibling = [(0, 1), (1, 0)]
    halves = partial_value.reshape(2, half, depth)
    keep = jnp.where(core == 0, halves[0], halves[1])
    give = jnp.where(core == 0, halves[1], halves[0])
    chip_half = keep + lax.ppermute(give, "dc", sibling)
    pieces = lax.all_to_all(
        chip_half.reshape(chips, half // chips, depth), "dy", 0, 0, tiled=True
    )
    summed = jnp.sum(pieces, axis=0)
    scale = lax.rsqrt(jnp.sum(summed * summed, axis=1, keepdims=True) + EPS)
    copies = jnp.broadcast_to(summed[None], pieces.shape) * jnp.broadcast_to(scale[None], (chips,) + scale.shape)
    own_half = lax.all_to_all(copies, "dy", 0, 0, tiled=True).reshape(half, depth)
    other_half = lax.ppermute(own_half, "dc", sibling)
    label_rows = jnp.where(
        core == 0,
        jnp.concatenate([own_half, other_half]),
        jnp.concatenate([other_half, own_half]),
    )

    starts = jnp.cumsum(cluster_sizes) - cluster_sizes
    cluster_ids = cluster_of(base + slots, starts)
    shard = jnp.arange(width, dtype=jnp.int32)
    first_id = cluster_of(shard * L_DEV, starts)
    last_id = cluster_of(shard * L_DEV + (L_DEV - 1), starts)

    half_ids = (
        cluster_of(base + core * half + jnp.arange(half), starts),
        cluster_of(base + (1 - core) * half + jnp.arange(half), starts),
    )
    local_sum = sum(
        jnp.dot(
            (cluster_ids[:, None] == ids[None, :]).astype(jnp.float32),
            rows,
            precision=lax.Precision.HIGH,
            preferred_element_type=jnp.float32,
        )
        for ids, rows in zip(half_ids, (own_half, other_half))
    )
    above = shard > here
    first_sum = jnp.sum(jnp.where((cluster_ids == first_id[here])[:, None], label_rows, 0.0), axis=0)
    last_sum = jnp.sum(jnp.where((cluster_ids == last_id[here])[:, None], label_rows, 0.0), axis=0)
    sending = jnp.where(above[:, None], last_sum[None, :], first_sum[None, :])
    lanes = 128
    gathered = lax.all_to_all(
        sending.reshape(width, -1, lanes), "label", 0, 0, tiled=True
    ).reshape(width, -1)

    doc_unit = unit_rows(features)
    own_scores, other_scores = (
        lax.dot_general(
            doc_unit,
            rows,
            (((1,), (1,)), ((), ())),
            precision=lax.Precision.HIGH,
            preferred_element_type=jnp.float32,
        )
        for rows in (own_half, other_half)
    )
    row_scores = jnp.where(
        core == 0,
        jnp.concatenate([own_scores, other_scores], axis=1),
        jnp.concatenate([other_scores, own_scores], axis=1),
    )
    below = shard < here
    take_below = (last_id[None, :] == cluster_ids[:, None]) & below[None, :]
    take_above = (first_id[None, :] == cluster_ids[:, None]) & above[None, :]
    weights = take_below | take_above
    cluster_sum = local_sum + jnp.dot(
        weights.astype(jnp.float32),
        gathered,
        precision=lax.Precision.HIGH,
        preferred_element_type=jnp.float32,
    )
    centroid = unit_rows(cluster_sum)
    return lax.dot_general(
        doc_unit,
        centroid,
        (((1,), (1,)), ((), ())),
        precision=lax.Precision.HIGH,
        preferred_element_type=jnp.float32,
    ) + row_scores


def solution(mesh):
    doc = mesh.shape["doc"]
    split = Mesh(mesh.devices.reshape(doc // 2, 2, -1), ("dy", "dc", "label"))
    docs = ("dy", "dc")
    in_specs = (P(docs, None), P(docs, None), P(), P())
    out_specs = P(docs, "label")
    return jax.shard_map(shards, mesh=split, in_specs=in_specs, out_specs=out_specs, check_vma=False)
```

```python
import jax
import jax.numpy as jnp
from jax import lax
from jax.sharding import Mesh, PartitionSpec as P

L_DEV = 256


EPS = 1e-06


def unit_rows(matrix):
    return matrix * lax.rsqrt(jnp.sum(matrix * matrix, axis=1, keepdims=True) + EPS)


def cluster_of(positions, starts):
    return jnp.sum((starts[None, 1:] <= positions[:, None]).astype(jnp.int32), axis=1)


def shards(features, doc_labels, tree_perm, cluster_sizes):
    width = lax.axis_size("label")
    here = lax.axis_index("label")
    base = here * L_DEV
    slots = jnp.arange(L_DEV, dtype=jnp.int32)

    own_perm = lax.dynamic_slice_in_dim(tree_perm, base, L_DEV)
    incidence = jnp.sum(
        (doc_labels.T[:, None, :] == own_perm[None, :, None]).astype(jnp.float32), axis=0
    )
    partial_value = jnp.dot(
        incidence, features, precision=lax.Precision.HIGH, preferred_element_type=jnp.float32
    )
    chips = lax.axis_size("dy")
    depth = features.shape[1]
    half = L_DEV // 2
    core = lax.axis_index("dc")
    sibling = [(0, 1), (1, 0)]
    keep = lax.dynamic_slice_in_dim(partial_value, core * half, half)
    give = lax.dynamic_slice_in_dim(partial_value, (1 - core) * half, half)
    chip_half = keep + lax.ppermute(give, "dc", sibling)
    pieces = lax.all_to_all(
        chip_half.reshape(chips, half // chips, depth), "dy", 0, 0, tiled=True
    )
    summed = jnp.sum(pieces, axis=0)
    scale = lax.rsqrt(jnp.sum(summed * summed, axis=1, keepdims=True) + EPS)
    copies = jnp.broadcast_to(summed[None], pieces.shape) * jnp.broadcast_to(scale[None], (chips,) + scale.shape)
    own_half = lax.all_to_all(copies, "dy", 0, 0, tiled=True).reshape(half, depth)
    other_half = lax.ppermute(own_half, "dc", sibling)

    starts = jnp.cumsum(cluster_sizes) - cluster_sizes
    cluster_ids = cluster_of(base + slots, starts)
    shard = jnp.arange(width, dtype=jnp.int32)
    first_id = cluster_of(shard * L_DEV, starts)
    last_id = cluster_of(shard * L_DEV + (L_DEV - 1), starts)

    half_ids = (
        cluster_of(base + core * half + jnp.arange(half), starts),
        cluster_of(base + (1 - core) * half + jnp.arange(half), starts),
    )
    local_sum = sum(
        jnp.dot(
            (cluster_ids[:, None] == ids[None, :]).astype(jnp.float32),
            rows,
            precision=lax.Precision.HIGH,
            preferred_element_type=jnp.float32,
        )
        for ids, rows in zip(half_ids, (own_half, other_half))
    )
    above = shard > here
    first_sum, last_sum = (
        sum(
            jnp.sum(jnp.where((ids == target)[:, None], rows, 0.0), axis=0)
            for ids, rows in zip(half_ids, (own_half, other_half))
        )
        for target in (first_id[here], last_id[here])
    )
    sending = jnp.where(above[:, None], last_sum[None, :], first_sum[None, :])
    lanes = 128
    gathered = lax.all_to_all(
        sending.reshape(width, -1, lanes), "label", 0, 0, tiled=True
    ).reshape(width, -1)

    doc_unit = unit_rows(features)
    own_scores, other_scores = (
        lax.dot_general(
            doc_unit,
            rows,
            (((1,), (1,)), ((), ())),
            precision=lax.Precision.HIGH,
            preferred_element_type=jnp.float32,
        )
        for rows in (own_half, other_half)
    )
    row_scores = jnp.where(
        core == 0,
        jnp.concatenate([own_scores, other_scores], axis=1),
        jnp.concatenate([other_scores, own_scores], axis=1),
    )
    below = shard < here
    take_below = (last_id[None, :] == cluster_ids[:, None]) & below[None, :]
    take_above = (first_id[None, :] == cluster_ids[:, None]) & above[None, :]
    weights = take_below | take_above
    cluster_sum = local_sum + jnp.dot(
        weights.astype(jnp.float32),
        gathered,
        precision=lax.Precision.HIGH,
        preferred_element_type=jnp.float32,
    )
    centroid = unit_rows(cluster_sum)
    return lax.dot_general(
        doc_unit,
        centroid,
        (((1,), (1,)), ((), ())),
        precision=lax.Precision.HIGH,
        preferred_element_type=jnp.float32,
    ) + row_scores


def solution(mesh):
    doc = mesh.shape["doc"]
    split = Mesh(mesh.devices.reshape(doc // 2, 2, -1), ("dy", "dc", "label"))
    docs = ("dy", "dc")
    in_specs = (P(docs, None), P(docs, None), P(), P())
    out_specs = P(docs, "label")
    return jax.shard_map(shards, mesh=split, in_specs=in_specs, out_specs=out_specs, check_vma=False)
```
